32 devices in a mesh: gx: 2 (over x), gy: 4 (over z), gz: 4 (over y, core).
Axes of the slice: x: 2, y: 2, z: 4, core: 2. Of those that a mesh axis runs over, the one named last changes fastest.
Arguments:
- spectrum: bfloat16 [64, 128, 32, 256], P('gx', 'gy', 'gz'), may hold values from 0.049804688 to 2
- wind_east: float32 [64, 128, 32], P('gx', 'gy', 'gz'), may hold values from -0.45 to 0.45
- wind_north: float32 [64, 128, 32], P('gx', 'gy', 'gz'), may hold values from -0.45 to 0.45
- fall_rate: float32 [32, 256], P('gz'), may hold values from 0.006 to 12
- cloud_cells: int32 [2, 4, 4, 64, 16], P('gx', 'gy', 'gz'), may hold values from 0 to 8191, as said below
- block_target: int32 [2, 4, 4, 64], P(None, None, 'gz'), may hold values from 0 to 8, as said below
- pair_inputs: bfloat16 [256, 2048], replicated, may hold values from -0.375 to 0.375
- pair_outputs: bfloat16 [1024, 256], replicated, may hold values from -0.1875 to 0.1875
- loss_kernel: bfloat16 [256, 256], replicated, may hold values from 0 to 0.00390625
- fragments: bfloat16 [256, 256], replicated, may hold values from 0 to 0.0078125
Outputs:
- settled: bfloat16 [64, 128, 32, 256], P('gx', 'gy', 'gz')
The draws below stay inside these ranges and needn't reach their ends.
Inputs may be any that keep to these rules, and one draw needn't show every extreme that they name: `cloud_cells`: entry [i, j, k, b, :] lists the local cell numbers (x * 32 + y) * 8 + z of block b of the device at mesh index (i, j, k); the 1024 entries of one device are distinct. `block_target`: entry [i, j, k, b] below 8 is the flat index i2 * (devices along gy) + j2 of the device (i2, j2, k) that works on block b of device (i, j, k); 8 marks a block without cloud. In each gz index the cloudy blocks number 8 * 32 in all, a device holds 1 to 64 of them, every device of the plane is named exactly 32 times, and by at most 8 blocks of any one device.
All inputs are finite; a program needn't handle non-finite values.
Results may differ from the reference program's by a relative error of at most 0.0032.
Values may be sent and summed in bfloat16 or wider, within the bound.
A program may use at most 128 MiB of HBM per device.

```python
import math
import jax
import jax.numpy as jnp
from jax import lax

SB = 256
PAIRS = 1024
CX = 32
CY = 32
CZ = 8
NB = 64
BLK = 16
RCAP = 32
PLANE = 8
NX = 64
NY = 128
NZ = 32
N_GX = 2
N_GY = 4
N_GZ = 4


def draw_fall_rate(key, part):
    keys = jax.random.split(jax.random.fold_in(key, 17), 4)
    terminal_speeds = jnp.exp(jax.random.uniform(keys[0], (SB,), jnp.float32, math.log(0.01), math.log(1.5)))
    air_density = jax.random.uniform(keys[1], (NZ, 1), jnp.float32, 0.8, 1.25)
    skipped_levels = jax.random.randint(keys[2], (3,), 0, NZ)
    vertical_levels = jnp.arange(NZ)
    breakup_events = 1.0 + 1.5 * jnp.sum((vertical_levels[:, None] == skipped_levels[None, :]).astype(jnp.float32), axis=1, keepdims=True)
    random_perturbation = jax.random.uniform(keys[3], (NZ, SB), jnp.float32, 0.85, 1.15)
    return (terminal_speeds[None, :] * air_density * breakup_events * random_perturbation).astype(jnp.float32)


def draw_cloud_cells(key, part):
    keys = jax.random.split(jax.random.fold_in(key, 3), N_GX * N_GY * N_GZ)

    def one_device(device_key):
        return jax.random.permutation(device_key, CX * CY * CZ)[:NB * BLK].astype(jnp.int32)
    listed = jax.vmap(one_device)(keys)
    return listed.reshape(N_GX, N_GY, N_GZ, NB, BLK)


def draw_block_target(key, part):
    plane_size = N_GX * N_GY
    total = plane_size * RCAP
    leftover = total - NB
    quota = leftover // (plane_size - 1)
    spare = leftover % (plane_size - 1)
    slope = (quota - 1) // (plane_size - 2)
    base_key = jax.random.fold_in(key, 5)

    def one_plane(plane_index):
        plane_key = jax.random.fold_in(base_key, plane_index)
        keys = jax.random.split(plane_key, 5)
        centre_row = jax.random.randint(keys[0], (), 0, N_GX)
        centre_column = jax.random.randint(keys[1], (), 0, N_GY)
        devices = jnp.arange(plane_size, dtype=jnp.int32)
        distance = jnp.abs(devices // N_GY - centre_row) + jnp.abs(devices % N_GY - centre_column)
        breaker = jax.random.permutation(keys[2], plane_size).astype(jnp.int32)
        scores = distance * plane_size + breaker
        ranking = jnp.argsort(jnp.argsort(scores)).astype(jnp.int32)
        loads = jnp.where(ranking == 0, NB, quota + slope * (plane_size - 2 * ranking) + (ranking - 1 < spare).astype(jnp.int32))
        starts = jnp.cumsum(loads) - loads
        device_keys = jax.random.split(keys[3], plane_size)
        logical = jax.vmap(lambda device_key: jax.random.permutation(device_key, NB).astype(jnp.int32))(device_keys)
        active = logical < loads[:, None]
        spread_target = (starts[:, None] + logical) % plane_size
        relabel = jax.random.permutation(keys[4], plane_size).astype(jnp.int32)
        return jnp.where(active, relabel[spread_target], plane_size).astype(jnp.int32)
    planes = jax.vmap(one_plane)(jnp.arange(N_GZ, dtype=jnp.int32))
    return planes.transpose(1, 0, 2).reshape(N_GX, N_GY, N_GZ, NB)


def block_scale(rng, dims, shards, smallest, largest):
    level, own = 1.0, jax.random.fold_in(rng, 6)
    for axis_at, parts in shards:
        heights = jnp.exp(jax.random.uniform(jax.random.fold_in(own, axis_at), (parts,), jnp.float32, smallest / len(shards), largest / len(shards)))
        level = level * jnp.repeat(heights, dims[axis_at] // parts).reshape([-1 if axis == axis_at else 1 for axis in range(len(dims))])
    return level


def noise(key, extent, spread, bound, held_as=jnp.bfloat16):
    return jnp.clip(spread * jax.random.normal(key, extent, jnp.float32), -bound, bound).astype(held_as)


def setup_inputs(seed: int = 0) -> dict:
    splits = jax.random.split(jax.random.key(seed), 11)
    return {
        "spectrum": jnp.clip(0.049804688 + 1.9501953 * jax.random.uniform(splits[0], (NX, NY, NZ, SB), jnp.float32) ** block_scale(splits[0], (NX, NY, NZ, SB), ((0, 2), (1, 4), (2, 4)), -0.2, 0.2), 0.049804688, 2.0).astype(jnp.bfloat16),
        "wind_east": jnp.clip(jax.random.uniform(splits[1], (NX, NY, NZ), jnp.float32, -0.45, 0.45) * block_scale(splits[1], (NX, NY, NZ), ((0, 2), (1, 4), (2, 4)), -0.4, 0.0), -0.45, 0.45),
        "wind_north": jnp.clip(jax.random.uniform(splits[2], (NX, NY, NZ), jnp.float32, -0.45, 0.45) * block_scale(splits[2], (NX, NY, NZ), ((0, 2), (1, 4), (2, 4)), -0.4, 0.0), -0.45, 0.45),
        "fall_rate": draw_fall_rate(jax.random.fold_in(splits[10], 71), 0),
        "cloud_cells": draw_cloud_cells(jax.random.fold_in(splits[10], 71), 0),
        "block_target": draw_block_target(jax.random.fold_in(splits[10], 71), 0),
        "pair_inputs": noise(splits[6], (SB, 2 * PAIRS), SB ** -0.5, 0.375),
        "pair_outputs": noise(splits[7], (PAIRS, SB), PAIRS ** -0.5, 0.1875),
        "loss_kernel": jnp.clip(jax.random.uniform(splits[8], (SB, SB), jnp.float32, 0.0, 0.00390625), 0.0, 0.00390625).astype(jnp.bfloat16),
        "fragments": jnp.clip(jax.random.uniform(splits[9], (SB, SB), jnp.float32, 0.0, 0.0078125), 0.0, 0.0078125).astype(jnp.bfloat16),
    }


def collide(cloud_rows, pair_inputs, pair_outputs, loss_kernel, fragments):
    pair_count = pair_outputs.shape[0]
    linear = jnp.dot(cloud_rows, pair_inputs, preferred_element_type=jnp.float32)
    products = (linear[:, :pair_count] * linear[:, pair_count:]).astype(jnp.bfloat16)
    decline = jnp.dot(cloud_rows, loss_kernel, preferred_element_type=jnp.float32)
    losses = cloud_rows.astype(jnp.float32) * decline
    gained = jnp.dot(products, pair_outputs, preferred_element_type=jnp.float32)
    gained = gained + jnp.dot(losses.astype(jnp.bfloat16), fragments, preferred_element_type=jnp.float32)
    return (gained - losses).astype(jnp.bfloat16)


def reference(spectrum, wind_east, wind_north, fall_rate, cloud_cells, block_target, pair_inputs, pair_outputs, loss_kernel, fragments):
    def slab_step(slab_index):
        first_level = slab_index * CZ
        values = lax.dynamic_slice_in_dim(spectrum, first_level, CZ, 2).astype(jnp.float32)
        east_rate = lax.dynamic_slice_in_dim(wind_east, first_level, CZ, 2)[..., None]
        north_rate = lax.dynamic_slice_in_dim(wind_north, first_level, CZ, 2)[..., None]
        from_west = jnp.roll(values, 1, 0)
        from_east = jnp.roll(values, -1, 0)
        from_south = jnp.roll(values, 1, 1)
        from_north = jnp.roll(values, -1, 1)
        advected = (values - jnp.maximum(east_rate, 0.0) * (values - from_west)
                    - jnp.minimum(east_rate, 0.0) * (from_east - values)
                    - jnp.maximum(north_rate, 0.0) * (values - from_south)
                    - jnp.minimum(north_rate, 0.0) * (from_north - values))
        targets = lax.dynamic_index_in_dim(block_target, slab_index, 2, keepdims=False).reshape(PLANE * NB)
        listed = lax.dynamic_index_in_dim(cloud_cells, slab_index, 2, keepdims=False).reshape(PLANE * NB, BLK)
        chosen = jnp.argsort((targets >= PLANE).astype(jnp.int32), stable=True)[: PLANE * RCAP].astype(jnp.int32)
        owners = chosen // NB
        tile_row = (owners // N_GY)[:, None]
        tile_column = (owners % N_GY)[:, None]
        local_ids = listed[chosen]
        cell_row = local_ids // (CY * CZ)
        cell_column = (local_ids // CZ) % CY
        cell_level = local_ids % CZ
        global_ids = (((tile_row * CX + cell_row) * NY + tile_column * CY + cell_column) * CZ + cell_level).reshape(-1).astype(jnp.int32)
        flat_values = advected.reshape(NX * NY * CZ, SB)
        gathered = flat_values[global_ids].astype(jnp.bfloat16)
        tendency = collide(gathered, pair_inputs, pair_outputs, loss_kernel, fragments)
        moist_field = flat_values.at[global_ids].add(tendency.astype(jnp.float32))
        return moist_field.reshape(NX, NY, CZ, SB)

    moist_slabs = lax.map(slab_step, jnp.arange(N_GZ, dtype=jnp.int32))
    fall_slabs = fall_rate.reshape(N_GZ, CZ, SB)

    def settle(inflow, pieces):
        moist_field, level_rates = pieces
        layers = [None] * CZ
        for level_index in reversed(range(CZ)):
            level_rate = level_rates[level_index]
            level_value = (moist_field[:, :, level_index] + inflow) / (1.0 + level_rate)
            inflow = level_rate * level_value
            layers[level_index] = level_value.astype(jnp.bfloat16)
        return inflow, jnp.stack(layers, axis=2)

    initial_flow = jnp.zeros((NX, NY, SB), jnp.float32)
    final_flow, settled = lax.scan(settle, initial_flow, (moist_slabs, fall_slabs), reverse=True)
    return settled.transpose(1, 2, 0, 3, 4).reshape(NX, NY, NZ, SB)
```

```python
import functools

import jax
import jax.numpy as jnp
from jax import lax
from jax.experimental import pallas as pl
from jax.experimental.pallas import tpu as pltpu
from jax.sharding import PartitionSpec as P

MESH = pl.DeviceIdType.MESH
F32 = jnp.float32
BF16 = jnp.bfloat16
I32 = jnp.int32
LANES = 128


def step_kernel(
    spec, winds_e, winds_n, fall_h, cells_h, target_h, pair_in_h, pair_out_h, loss_h, frag_h,
    adv, moist, arrived, edge_in,
    local, we, wn, west, east, south, north, fall, cells, cells_v, target, pair_in, pair_out, loss, frag,
    rows, q, pz, ids, parts_p, flux, edge_flux, extra,
    load_sem, in_sem, send_sem, recv_sem, down_sem, got_sem,
):
    nx, ny, packed, _ = spec.shape
    nz, bins = fall.shape
    halves = bins // LANES
    width, blocks = cells.shape
    total = width * blocks
    pairs = pair_out.shape[0]
    parts = load_sem.shape[0]
    per = nx // parts
    gx, gy, me = lax.axis_index("gx"), lax.axis_index("gy"), lax.axis_index("gz")
    sx, sy, count = lax.axis_size("gx"), lax.axis_size("gy"), lax.axis_size("gz")
    plane = sx * sy
    top = count - 1
    to_west = {"gx": lax.rem(gx + sx - 1, sx)}
    to_east = {"gx": lax.rem(gx + 1, sx)}
    to_south = {"gy": lax.rem(gy + sy - 1, sy)}
    to_north = {"gy": lax.rem(gy + 1, sy)}
    above = {"gz": lax.rem(me + 1, count)}
    below = {"gz": lax.rem(me + top, count)}

    barrier = pltpu.get_barrier_semaphore()
    for peer in (to_west, to_east, to_south, to_north, above, below):
        pl.semaphore_signal(barrier, inc=1, device_id=peer, device_id_type=MESH)

    def fetch(i, src, dst):
        return pltpu.make_async_copy(src, dst, in_sem.at[i])

    wind_loads = [fetch(0, winds_e, we), fetch(1, winds_n, wn)]
    loads = [
        pltpu.make_async_copy(spec.at[pl.ds(p * per, per)], local.at[pl.ds(1 + p * per, per)], load_sem.at[p])
        for p in range(parts)
    ]
    small = [fetch(2, fall_h, fall), fetch(3, cells_h, cells), fetch(4, cells_h, cells_v), fetch(5, target_h, target)]
    weights = [
        fetch(6, pair_in_h, pair_in), fetch(7, pair_out_h, pair_out), fetch(8, loss_h, loss), fetch(9, frag_h, frag)
    ]
    for load in wind_loads + loads + small + weights:
        load.start()
    pl.semaphore_wait(barrier, 6)

    sends = [
        pltpu.make_async_remote_copy(
            src_ref=src,
            dst_ref=dst,
            send_sem=send_sem.at[i],
            recv_sem=recv_sem.at[i],
            device_id=peer,
            device_id_type=MESH,
        )
        for i, (src, dst, peer) in enumerate(
            (
                (spec.at[:, ny - 1], south, to_north),
                (spec.at[:, 0], north, to_south),
                (spec.at[nx - 1], west, to_east),
                (spec.at[0], east, to_west),
            )
        )
    ]
    for send in sends:
        send.start()

    zero_row = jnp.zeros((ny, packed, LANES), BF16)
    local[0] = zero_row
    local[nx + 1] = zero_row

    def spread(column):
        wide = jnp.broadcast_to(column, (nz, LANES))
        return jnp.concatenate([wide] * halves, axis=0).astype(BF16)

    def one_row(x, carry):
        east_w, north_w = we[x], wn[x]
        zero = jnp.zeros((packed, LANES), BF16)
        behind = zero
        centre = local[x + 1, 0]
        for y in range(ny):
            ahead = local[x + 1, y + 1] if y + 1 < ny else zero
            a, b = spread(east_w[:, y : y + 1]), spread(north_w[:, y : y + 1])
            up_x = jnp.where(a > 0, local[x, y], local[x + 2, y])
            up_y = jnp.where(b > 0, behind, ahead)
            change = jnp.abs(a) * (up_x - centre) + jnp.abs(b) * (up_y - centre)
            value = centre.astype(F32) + change.astype(F32)
            at = pl.ds(pl.multiple_of((x * ny + y) * nz, nz), nz)
            for h in range(halves):
                adv[h, at, :] = value[h * nz : (h + 1) * nz]
            behind, centre = centre, ahead
        return carry

    for load in wind_loads:
        load.wait()
    done = 0
    for p in range(parts):
        loads[p].wait()
        upto = nx if p == parts - 1 else (p + 1) * per - 1
        lax.fori_loop(done, upto, one_row, 0)
        done = upto

    for load in small:
        load.wait()

    ratio = fall[...] / (1.0 + fall[...])
    share = jnp.ones((1, bins), F32)
    for z in range(nz):
        share = share * ratio[z : z + 1, :]
        parts_p[z : z + 1, :] = share
    parts_p[nz : 2 * nz, :] = ratio
    gain = share

    listed = cells_v[...]
    cloudy = target[gx, gy] < plane
    columns = jnp.where(cloudy, listed // nz, -1)
    per_tile = LANES // blocks
    for t in range(total // LANES):
        ids[t : t + 1, :] = jnp.concatenate(
            [columns[t * per_tile + i : t * per_tile + i + 1, :] for i in range(per_tile)], axis=1
        )
    heights = (listed % nz).astype(F32).T
    high = parts_p[0:nz, :].astype(BF16)
    low = (parts_p[0:nz, :] - high.astype(F32)).astype(BF16)
    table = jnp.concatenate([high, low, jnp.zeros((LANES - 2 * nz, bins), BF16)], axis=0)
    lane = lax.broadcasted_iota(I32, (blocks, LANES), 1)
    level_of = jnp.where(lane < 2 * nz, lane % nz, -1).astype(F32)
    for j in range(width):
        pick = jnp.where(jnp.broadcast_to(heights[:, j : j + 1], (blocks, LANES)) == level_of, 1.0, 0.0).astype(BF16)
        pz[j * blocks : (j + 1) * blocks, :] = jnp.dot(pick, table, preferred_element_type=F32)

    for load in weights:
        load.wait()

    def gather(k, carry):
        for j in range(width):
            cell = pl.ds(cells[j, k], 1)
            for h in range(halves):
                rows[h, pl.ds(j * blocks + k, 1), :] = adv[h, cell, :]
        return carry

    size = min(256, total)
    tile = min(256, pairs)

    def collide(i, carry):
        at = pl.ds(pl.multiple_of(i * size, size), size)
        full = jnp.concatenate([rows[h, at, :] for h in range(halves)], axis=1)
        row = full.astype(BF16)
        decline = jnp.dot(row, loss[...], preferred_element_type=F32)
        losses = row.astype(F32) * decline
        gained = jnp.dot(losses.astype(BF16), frag[...], preferred_element_type=F32)
        for n in range(0, pairs, tile):
            first = jnp.dot(row, pair_in[:, n : n + tile], preferred_element_type=F32)
            second = jnp.dot(row, pair_in[:, pairs + n : pairs + n + tile], preferred_element_type=F32)
            product = (first * second).astype(BF16)
            gained = gained + jnp.dot(product, pair_out[n : n + tile, :], preferred_element_type=F32)
        tendency = (gained - losses).astype(BF16).astype(F32)
        q[at, :] = (tendency * pz[at, :]).astype(BF16)
        after = full + tendency
        for h in range(halves):
            moist[h, at, :] = after[:, h * LANES : (h + 1) * LANES]
        return carry

    def collide_all():
        lax.fori_loop(0, blocks, gather, 0)
        lax.fori_loop(0, total // size, collide, 0)

    def collected(column):
        hot = [
            jnp.where(jnp.broadcast_to(ids[t : t + 1, :], column.shape) == column, 1.0, 0.0).astype(BF16)
            for t in range(total // LANES)
        ]
        return jnp.dot(jnp.concatenate(hot, axis=1), q[...], preferred_element_type=F32)

    def drained(base, stride, at_lanes, h):
        inflow = jnp.zeros((8, LANES), F32)
        for z in reversed(range(nz)):
            level = adv[h, pl.ds(base + z, 8, stride=stride), :]
            inflow = (level + inflow) * parts_p[nz + z : nz + z + 1, at_lanes]
        return inflow

    inner = down_sem.shape[0] - 1
    span = (nx - 2) // inner
    wide = span * ny

    def down(p):
        src = edge_flux if p == inner else flux.at[pl.ds(p * wide, wide)]
        dst = edge_in if p == inner else arrived.at[pl.ds((1 + p * span) * ny, wide)]
        return pltpu.make_async_remote_copy(
            src_ref=src,
            dst_ref=dst,
            send_sem=down_sem.at[p],
            recv_sem=got_sem.at[p],
            device_id={"gz": jnp.maximum(me - 1, 0)},
            device_id_type=MESH,
        )

    def relay(p):
        down(p).wait_recv()

        @pl.when(me > 0)
        def _():
            if p == inner:
                edge_flux[...] = (edge_flux[...].astype(F32) + edge_in[...].astype(F32) * gain).astype(BF16)
            else:
                at = pl.ds(p * wide, wide)
                got = arrived[pl.ds((1 + p * span) * ny, wide), :].astype(F32)
                flux[at, :] = (flux[at, :].astype(F32) + got * gain).astype(BF16)
            down(p).start()

    collide_all()

    for p in range(inner):
        column = lax.broadcasted_iota(I32, (wide, LANES), 0) + (1 + p * span) * ny
        extra[0:wide, :] = collected(column)

        def drain(g, carry):
            at = pl.ds(pl.multiple_of(g * 8, 8), 8)
            base = pl.multiple_of(((1 + p * span) * ny + g * 8) * nz, 8 * nz)
            for h in range(halves):
                lanes = slice(h * LANES, (h + 1) * LANES)
                extra[at, lanes] = extra[at, lanes] + drained(base, nz, lanes, h)
            return carry

        lax.fori_loop(0, wide // 8, drain, 0, unroll=4)
        flux[p * wide : (p + 1) * wide, :] = extra[0:wide, :].astype(BF16)

        @pl.when(me == top)
        def _():
            down(p).start()

        @pl.when(me == top - 1)
        def _():
            relay(p)

    for send in sends[:2]:
        send.wait_recv()

    def edges(x, carry):
        for y, halo, sign in ((0, south, 1.0), (ny - 1, north, -1.0)):
            wind = jnp.maximum(sign * jnp.broadcast_to(wn[x][:, y : y + 1], (nz, LANES)), 0.0)
            at = pl.ds(pl.multiple_of((x * ny + y) * nz, nz), nz)
            came = halo[x].astype(F32)
            for h in range(halves):
                adv[h, at, :] = adv[h, at, :] + wind * came[h * nz : (h + 1) * nz]
        return carry

    lax.fori_loop(0, nx, edges, 0, unroll=4)

    for send, x, halo, sign in ((sends[2], 0, west, 1.0), (sends[3], nx - 1, east, -1.0)):
        send.wait_recv()
        wind = jnp.maximum(sign * we[x], 0.0)
        for y in range(ny):
            at = pl.ds((x * ny + y) * nz, nz)
            spread_wind = jnp.broadcast_to(wind[:, y : y + 1], (nz, LANES))
            came = halo[y].astype(F32)
            for h in range(halves):
                adv[h, at, :] = adv[h, at, :] + spread_wind * came[h * nz : (h + 1) * nz]

    collide_all()

    rim = edge_flux.shape[0]
    order = lax.broadcasted_iota(I32, (rim, LANES), 0)
    near = jnp.where(order < ny, order, order - ny + (nx - 1) * ny)
    far = order - 2 * ny
    side = jnp.where(far < nx, far * ny, (far - nx) * ny + ny - 1)
    extra[0:rim, :] = collected(jnp.where(order < 2 * ny, near, side))
    for g in range(rim // 8):
        r = g * 8
        if r < 2 * ny:
            x, y = (0, r) if r < ny else (nx - 1, r - ny)
            base, stride = (x * ny + y) * nz, nz
        else:
            x, y = (r - 2 * ny, 0) if r - 2 * ny < nx else (r - 2 * ny - nx, ny - 1)
            base, stride = (x * ny + y) * nz, ny * nz
        for h in range(halves):
            lanes = slice(h * LANES, (h + 1) * LANES)
            extra[r : r + 8, lanes] = extra[r : r + 8, lanes] + drained(base, stride, lanes, h)
    edge_flux[...] = extra[0:rim, :].astype(BF16)

    @pl.when(me == top)
    def _():
        down(inner).start()
        arrived[...] = jnp.zeros(arrived.shape, BF16)
        edge_in[...] = jnp.zeros(edge_in.shape, BF16)

    @pl.when(me == top - 1)
    def _():
        relay(inner)

    @pl.when(me < top - 1)
    def _():
        for p in range(inner + 1):
            relay(p)

    @pl.when(me > 0)
    def _():
        for p in range(inner + 1):
            down(p).wait_send()

    for send in sends:
        send.wait_send()


def settle_kernel(
    adv_in, moist, arrived, edge_in, cells, target, fall, adv, out, flow, inverse, level_out, staged, out_sem
):
    nx, ny, packed, _ = out.shape
    nz, bins = fall.shape
    halves = bins // LANES
    width, blocks = cells.shape
    plane = target.shape[0] * target.shape[1]
    gx, gy = lax.axis_index("gx"), lax.axis_index("gy")

    inverse[...] = 1.0 / (1.0 + fall[...])
    flow[...] = arrived[...].astype(F32)
    rim = edge_in[...].astype(F32)
    flow[0:ny, :] = rim[0:ny]
    flow[(nx - 1) * ny : nx * ny, :] = rim[ny : 2 * ny]
    for i in range(nx):
        flow[i * ny : i * ny + 1, :] = rim[2 * ny + i : 2 * ny + i + 1]
        flow[i * ny + ny - 1 : i * ny + ny, :] = rim[2 * ny + nx + i : 2 * ny + nx + i + 1]

    def scatter(k, carry):
        @pl.when(target[gx, gy, 0, k] < plane)
        def _():
            for j in range(width):
                cell = pl.ds(cells[j, k], 1)
                for h in range(halves):
                    adv[h, cell, :] = moist[h, pl.ds(j * blocks + k, 1), :]

        return carry

    lax.fori_loop(0, blocks, scatter, 0)

    def push(x, slot):
        return pltpu.make_async_copy(staged.at[slot], out.at[x], out_sem.at[slot])

    slots = staged.shape[0]

    def row(x, carry):
        slot = lax.rem(x, slots)
        for g in range(ny // 8):
            base = pl.multiple_of((x * ny + g * 8) * nz, 8 * nz)
            at = pl.ds(pl.multiple_of(x * ny + g * 8, 8), 8)
            for h in range(halves):
                lanes = slice(h * LANES, (h + 1) * LANES)
                inflow = flow[at, lanes]
                for z in reversed(range(nz)):
                    level = adv[h, pl.ds(base + z, 8, stride=nz), :]
                    value = (level + inflow) * inverse[z : z + 1, lanes]
                    level_out[h, pl.ds(g * 8 * nz + z, 8, stride=nz), :] = value
                    inflow = value * fall[z : z + 1, lanes]

        @pl.when(x >= slots)
        def _():
            push(x - slots, slot).wait()

        for y in range(ny):
            pieces = [level_out[h, y * nz : (y + 1) * nz, :] for h in range(halves)]
            staged[slot, y] = jnp.concatenate(pieces, axis=0).astype(BF16)
        push(x, slot).start()
        return carry

    lax.fori_loop(0, nx, row, 0)
    for x in range(nx - slots, nx):
        push(x, x % slots).wait()


def body(
    spectrum,
    wind_east,
    wind_north,
    fall_rate,
    cloud_cells,
    block_target,
    pair_inputs,
    pair_outputs,
    loss_kernel,
    fragments,
):
    nx, ny, nz, bins = spectrum.shape
    halves = bins // LANES
    cells = nx * ny * nz
    columns = nx * ny
    blocks, width = cloud_cells.shape[3], cloud_cells.shape[4]
    total = blocks * width
    pairs = pair_outputs.shape[0]
    packed = nz * halves
    winds = (wind_east.transpose(0, 2, 1), wind_north.transpose(0, 2, 1))
    listed = cloud_cells.reshape(blocks, width).T
    dma = pltpu.SemaphoreType.DMA
    hbm = pl.BlockSpec(memory_space=pltpu.HBM)
    smem = pl.BlockSpec(memory_space=pltpu.SMEM)
    vmem = pl.BlockSpec(memory_space=pltpu.VMEM)
    dense = spectrum.reshape(nx, ny, nz, halves, LANES).transpose(0, 1, 3, 2, 4).reshape(nx, ny, packed, LANES)
    span = max(s for s in range(1, 7) if (nx - 2) % s == 0)
    inner = (nx - 2) // span
    rim = 2 * (nx + ny)
    parts = 4

    adv, moist, arrived, edge_in = pl.pallas_call(
        step_kernel,
        out_shape=(
            pltpu.VMEM((halves, cells, LANES), F32),
            pltpu.VMEM((halves, total, LANES), F32),
            pltpu.VMEM((columns, bins), BF16),
            pltpu.VMEM((rim, bins), BF16),
        ),
        in_specs=[hbm] * 10,
        out_specs=(vmem,) * 4,
        scratch_shapes=[
            pltpu.VMEM((nx + 2, ny, packed, LANES), BF16),
            pltpu.VMEM(winds[0].shape, F32),
            pltpu.VMEM(winds[1].shape, F32),
            pltpu.VMEM((ny, packed, LANES), BF16),
            pltpu.VMEM((ny, packed, LANES), BF16),
            pltpu.VMEM((nx, packed, LANES), BF16),
            pltpu.VMEM((nx, packed, LANES), BF16),
            pltpu.VMEM(fall_rate.shape, F32),
            pltpu.SMEM((width, blocks), I32),
            pltpu.VMEM((width, blocks), I32),
            pltpu.VMEM(block_target.shape, I32),
            pltpu.VMEM(pair_inputs.shape, BF16),
            pltpu.VMEM(pair_outputs.shape, BF16),
            pltpu.VMEM(loss_kernel.shape, BF16),
            pltpu.VMEM(fragments.shape, BF16),
            pltpu.VMEM((halves, total, LANES), F32),
            pltpu.VMEM((total, bins), BF16),
            pltpu.VMEM((total, bins), F32),
            pltpu.VMEM((max(total // LANES, 8), LANES), I32),
            pltpu.VMEM((2 * nz, bins), F32),
            pltpu.VMEM(((nx - 2) * ny, bins), BF16),
            pltpu.VMEM((rim, bins), BF16),
            pltpu.VMEM((max(span * ny, rim), bins), F32),
            dma((parts,)),
            dma((10,)),
            dma((4,)),
            dma((4,)),
            dma((inner + 1,)),
            dma((inner + 1,)),
        ],
        compiler_params=pltpu.CompilerParams(
            collective_id=0, has_side_effects=True, vmem_limit_bytes=(60 << 20) - cells * bins * 4
        ),
        name="step",
    )(dense, *winds, fall_rate, listed, block_target, pair_inputs, pair_outputs, loss_kernel, fragments)

    slots = 4
    _, settled = pl.pallas_call(
        settle_kernel,
        out_shape=(
            pltpu.VMEM((halves, cells, LANES), F32),
            jax.ShapeDtypeStruct((nx, ny, packed, LANES), BF16),
        ),
        in_specs=[vmem] * 4 + [smem, smem, vmem],
        out_specs=(vmem, hbm),
        scratch_shapes=[
            pltpu.VMEM((columns, bins), F32),
            pltpu.VMEM((nz, bins), F32),
            pltpu.VMEM((halves, ny * nz, LANES), F32),
            pltpu.VMEM((slots, ny, packed, LANES), BF16),
            dma((slots,)),
        ],
        input_output_aliases={0: 0},
        compiler_params=pltpu.CompilerParams(vmem_limit_bytes=32 << 20),
        name="settle",
    )(adv, moist, arrived, edge_in, listed, block_target, fall_rate)
    return settled.reshape(nx, ny, halves, nz, LANES).transpose(0, 1, 3, 2, 4).reshape(nx, ny, nz, bins)


def solution(mesh):
    in_specs = (
        P("gx", "gy", "gz", None),
        P("gx", "gy", "gz"),
        P("gx", "gy", "gz"),
        P("gz", None),
        P("gx", "gy", "gz", None, None),
        P(None, None, "gz", None),
        P(),
        P(),
        P(),
        P(),
    )
    out_specs = P("gx", "gy", "gz", None)
    return jax.shard_map(body, mesh=mesh, in_specs=in_specs, out_specs=out_specs, check_vma=False)
```

```python
import functools

import jax
import jax.numpy as jnp
from jax import lax
from jax.experimental import pallas as pl
from jax.experimental.pallas import tpu as pltpu
from jax.sharding import PartitionSpec as P

MESH = pl.DeviceIdType.MESH
F32 = jnp.float32
BF16 = jnp.bfloat16
I32 = jnp.int32
LANES = 128
GROUP = 8


def spot_of(column, level, levels):
    return (column // GROUP * levels + level) * GROUP + column % GROUP


def step_kernel(
    spec, winds_e, winds_n, fall_h, cells_h, target_h, pair_in_h, pair_out_h, loss_h, frag_h,
    adv, moist, arrived, edge_in, spots, fall,
    local, we, wn, west, east, south, north, cells, listed_v, target, pair_in, pair_out, loss, frag,
    rows, q, pz, ids, live, shares, settled, flux, edge_flux, extra,
    load_sem, in_sem, spot_sem, send_sem, recv_sem, down_sem, got_sem,
):
    nx, ny, packed, _ = spec.shape
    nz, bins = fall.shape
    halves = bins // LANES
    width, blocks = cells.shape
    total = width * blocks
    pairs = pair_out.shape[0]
    parts = load_sem.shape[0]
    per = nx // parts
    gx, gy, me = lax.axis_index("gx"), lax.axis_index("gy"), lax.axis_index("gz")
    sx, sy, count = lax.axis_size("gx"), lax.axis_size("gy"), lax.axis_size("gz")
    plane = sx * sy
    top = count - 1
    to_west = {"gx": lax.rem(gx + sx - 1, sx)}
    to_east = {"gx": lax.rem(gx + 1, sx)}
    to_south = {"gy": lax.rem(gy + sy - 1, sy)}
    to_north = {"gy": lax.rem(gy + 1, sy)}
    above = {"gz": lax.rem(me + 1, count)}
    below = {"gz": lax.rem(me + top, count)}

    barrier = pltpu.get_barrier_semaphore()
    for peer in (to_west, to_east, to_south, to_north, above, below):
        pl.semaphore_signal(barrier, inc=1, device_id=peer, device_id_type=MESH)

    def fetch(i, src, dst):
        return pltpu.make_async_copy(src, dst, in_sem.at[i])

    wind_loads = [fetch(0, winds_e, we), fetch(1, winds_n, wn)]
    loads = [
        pltpu.make_async_copy(spec.at[pl.ds(p * per, per)], local.at[pl.ds(1 + p * per, per)], load_sem.at[p])
        for p in range(parts)
    ]
    small = [fetch(2, fall_h, fall), fetch(3, cells_h, listed_v), fetch(4, target_h, target)]
    weights = [
        fetch(6, pair_in_h, pair_in), fetch(7, pair_out_h, pair_out), fetch(8, loss_h, loss), fetch(9, frag_h, frag)
    ]
    for load in wind_loads + loads + small + weights:
        load.start()
    pl.semaphore_wait(barrier, 6)

    sends = [
        pltpu.make_async_remote_copy(
            src_ref=src,
            dst_ref=dst,
            send_sem=send_sem.at[i],
            recv_sem=recv_sem.at[i],
            device_id=peer,
            device_id_type=MESH,
        )
        for i, (src, dst, peer) in enumerate(
            (
                (spec.at[:, ny - 1], south, to_north),
                (spec.at[:, 0], north, to_south),
                (spec.at[nx - 1], west, to_east),
                (spec.at[0], east, to_west),
            )
        )
    ]
    for send in sends:
        send.start()

    zero_row = jnp.zeros((ny, packed, LANES), BF16)
    local[0] = zero_row
    local[nx + 1] = zero_row

    def stacked(tile):
        return jnp.concatenate([tile] * halves, axis=0).astype(BF16)

    def spread(tile, y):
        return jnp.broadcast_to(tile[:, y : y + 1], (packed, LANES))

    def one_row(x, carry):
        east_w, north_w = stacked(we[x]), stacked(wn[x])
        zero = jnp.zeros((packed, LANES), BF16)
        behind = zero
        centre = local[x + 1, 0]
        for y in range(ny):
            ahead = local[x + 1, y + 1] if y + 1 < ny else zero
            a, b = spread(east_w, y), spread(north_w, y)
            up_x = jnp.where(a > 0, local[x, y], local[x + 2, y])
            up_y = jnp.where(b > 0, behind, ahead)
            change = jnp.abs(a) * (up_x - centre) + jnp.abs(b) * (up_y - centre)
            value = centre.astype(F32) + change.astype(F32)
            base = pl.multiple_of((x * ny + y - y % GROUP) * nz, GROUP * nz)
            for h in range(halves):
                adv[h, pl.ds(base + y % GROUP, nz, stride=GROUP), :] = value[h * nz : (h + 1) * nz]
            behind, centre = centre, ahead
        return carry

    for load in small:
        load.wait()

    ratio = fall[...] / (1.0 + fall[...])
    share = jnp.ones((1, bins), F32)
    for z in range(nz):
        share = share * ratio[z : z + 1, :]
        shares[z : z + 1, :] = share
    shares[nz : 2 * nz, :] = ratio
    gain = share

    listed = listed_v[...]
    spots[...] = spot_of(listed // nz, listed % nz, nz)
    spot = pltpu.make_async_copy(spots, cells, spot_sem.at[0])
    spot.start()
    cloudy = target[gx, gy] < plane
    columns = jnp.where(cloudy, listed // nz, -1)
    per_tile = LANES // blocks
    for t in range(total // LANES):
        ids[t : t + 1, :] = jnp.concatenate(
            [columns[t * per_tile + i : t * per_tile + i + 1, :] for i in range(per_tile)], axis=1
        )
    flags = jnp.broadcast_to(jnp.where(cloudy, 1.0, 0.0), (8, blocks)).T
    live[...] = jnp.broadcast_to(flags[:, 0:1], (blocks, LANES))
    heights = (listed % nz).astype(F32).T
    high = shares[0:nz, :].astype(BF16)
    low = (shares[0:nz, :] - high.astype(F32)).astype(BF16)
    table = jnp.concatenate([high, low, jnp.zeros((LANES - 2 * nz, bins), BF16)], axis=0)
    lane = lax.broadcasted_iota(I32, (blocks, LANES), 1)
    level_of = jnp.where(lane < 2 * nz, lane % nz, -1).astype(F32)
    picks = [
        jnp.where(jnp.broadcast_to(heights[:, j : j + 1], (blocks, LANES)) == level_of, 1.0, 0.0).astype(BF16)
        for j in range(width)
    ]
    pz[...] = jnp.dot(jnp.concatenate(picks, axis=0), table, preferred_element_type=F32)
    for load in wind_loads:
        load.wait()
    done = 0
    for p in range(parts):
        loads[p].wait()
        upto = nx if p == parts - 1 else (p + 1) * per - 1
        lax.fori_loop(done, upto, one_row, 0)
        done = upto

    for load in weights:
        load.wait()

    size = min(256, total)
    tile = min(256, pairs)
    inner = down_sem.shape[0] - 1
    span = (nx - 2) // inner
    wide = span * ny

    def gather(i):
        for r in range(i * size, (i + 1) * size):
            cell = pl.ds(cells[r // blocks, r % blocks], 1)
            for h in range(halves):
                rows[h, r : r + 1, :] = adv[h, cell, :]

    def collide(i):
        at = slice(i * size, (i + 1) * size)
        full = jnp.concatenate([rows[h, at, :] for h in range(halves)], axis=1)
        row = full.astype(BF16)
        decline = jnp.dot(row, loss[...], preferred_element_type=F32)
        losses = row.astype(F32) * decline
        gained = jnp.dot(losses.astype(BF16), frag[...], preferred_element_type=F32)
        for n in range(0, pairs, tile):
            first = jnp.dot(row, pair_in[:, n : n + tile], preferred_element_type=F32)
            second = jnp.dot(row, pair_in[:, pairs + n : pairs + n + tile], preferred_element_type=F32)
            product = (first * second).astype(BF16)
            gained = gained + jnp.dot(product, pair_out[n : n + tile, :], preferred_element_type=F32)
        tendency = (gained - losses).astype(BF16).astype(F32)
        alive = jnp.concatenate([jnp.concatenate([live[...]] * halves, axis=1)] * (size // blocks), axis=0)
        tendency = jnp.where(alive > 0.0, tendency, 0.0)
        q[at, :] = (tendency * pz[at, :]).astype(BF16)
        after = full + tendency
        for h in range(halves):
            moist[h, at, :] = after[:, h * LANES : (h + 1) * LANES]

    def total_of(terms):
        while len(terms) > 1:
            terms = [a + b for a, b in zip(terms[::2], terms[1::2])]
        return terms[0]

    def sink(x):
        for g in range(x * ny // GROUP, (x + 1) * ny // GROUP):
            at = slice(g * GROUP - ny, (g + 1) * GROUP - ny)
            for h in range(halves):
                lanes = slice(h * LANES, (h + 1) * LANES)
                terms = [
                    adv[h, (g * nz + z) * GROUP : (g * nz + z + 1) * GROUP, :] * shares[z : z + 1, lanes]
                    for z in range(nz)
                ]
                settled[at, lanes] = total_of(terms)

    def collide_all(also):
        chunks = total // size
        gather(0)
        for i in range(chunks):
            if i + 1 < chunks:
                gather(i + 1)
            if also:
                for x in range(1 + i * (nx - 2) // chunks, 1 + (i + 1) * (nx - 2) // chunks):
                    sink(x)
            collide(i)

    def collected(column):
        hot = [
            jnp.where(jnp.broadcast_to(ids[t : t + 1, :], column.shape) == column, 1.0, 0.0).astype(BF16)
            for t in range(total // LANES)
        ]
        return jnp.dot(jnp.concatenate(hot, axis=1), q[...], preferred_element_type=F32)

    def drained(column, apart, lanes, h):
        first = spot_of(column, 0, nz)
        stride = 1 if apart == 1 else apart * nz
        terms = [
            adv[h, pl.ds(first + z * GROUP, GROUP, stride=stride), :] * shares[z : z + 1, lanes] for z in range(nz)
        ]
        return total_of(terms)

    def down(p):
        src = edge_flux if p == inner else flux.at[pl.ds(p * wide, wide)]
        dst = edge_in if p == inner else arrived.at[pl.ds((1 + p * span) * ny, wide)]
        return pltpu.make_async_remote_copy(
            src_ref=src,
            dst_ref=dst,
            send_sem=down_sem.at[p],
            recv_sem=got_sem.at[p],
            device_id={"gz": jnp.maximum(me - 1, 0)},
            device_id_type=MESH,
        )

    def relay(p):
        down(p).wait_recv()

        @pl.when(me > 0)
        def _():
            if p == inner:
                edge_flux[...] = (edge_flux[...].astype(F32) + edge_in[...].astype(F32) * gain).astype(BF16)
            else:
                at = pl.ds(p * wide, wide)
                got = arrived[pl.ds((1 + p * span) * ny, wide), :].astype(F32)
                flux[at, :] = (flux[at, :].astype(F32) + got * gain).astype(BF16)
            down(p).start()

    spot.wait()
    collide_all(True)

    for p in range(inner):
        column = lax.broadcasted_iota(I32, (wide, LANES), 0) + (1 + p * span) * ny
        at = slice(p * wide, (p + 1) * wide)
        flux[at, :] = (collected(column) + settled[at, :]).astype(BF16)

        @pl.when(me == top)
        def _():
            down(p).start()

        @pl.when(me == top - 1)
        def _():
            relay(p)

    for send in sends[:2]:
        send.wait_recv()

    def add_halo(column, wind, halo):
        came = wind.astype(F32) * halo.astype(F32)
        at = pl.ds(spot_of(column, 0, nz), nz, stride=GROUP)
        for h in range(halves):
            adv[h, at, :] = adv[h, at, :] + came[h * nz : (h + 1) * nz]

    def edges(x, carry):
        winds = stacked(wn[x])
        add_halo(x * ny, jnp.maximum(spread(winds, 0), 0), south[x])
        add_halo(x * ny + ny - 1, jnp.maximum(-spread(winds, ny - 1), 0), north[x])
        return carry

    lax.fori_loop(0, nx, edges, 0, unroll=8)

    for send, x, halo, sign in ((sends[2], 0, west, 1.0), (sends[3], nx - 1, east, -1.0)):
        send.wait_recv()
        winds = jnp.maximum(sign * stacked(we[x]), 0)
        for y in range(ny):
            add_halo(x * ny + y, spread(winds, y), halo[y])

    collide_all(False)

    rim = edge_flux.shape[0]
    order = lax.broadcasted_iota(I32, (rim, LANES), 0)
    near = jnp.where(order < ny, order, order - ny + (nx - 1) * ny)
    far = order - 2 * ny
    side = jnp.where(far < nx, far * ny, (far - nx) * ny + ny - 1)
    extra[0:rim, :] = collected(jnp.where(order < 2 * ny, near, side))
    for r in range(0, rim, GROUP):
        if r < 2 * ny:
            x, y = (0, r) if r < ny else (nx - 1, r - ny)
            base, stride = x * ny + y, 1
        else:
            x, y = (r - 2 * ny, 0) if r - 2 * ny < nx else (r - 2 * ny - nx, ny - 1)
            base, stride = x * ny + y, ny
        for h in range(halves):
            lanes = slice(h * LANES, (h + 1) * LANES)
            extra[r : r + GROUP, lanes] = extra[r : r + GROUP, lanes] + drained(base, stride, lanes, h)
    edge_flux[...] = extra[0:rim, :].astype(BF16)

    @pl.when(me == top)
    def _():
        down(inner).start()
        arrived[...] = jnp.zeros(arrived.shape, BF16)
        edge_in[...] = jnp.zeros(edge_in.shape, BF16)

    @pl.when(me == top - 1)
    def _():
        relay(inner)

    @pl.when(me < top - 1)
    def _():
        for p in range(inner + 1):
            relay(p)

    @pl.when(me > 0)
    def _():
        for p in range(inner + 1):
            down(p).wait_send()

    for send in sends:
        send.wait_send()


def settle_kernel(
    adv_in, moist, arrived, edge_in, spots, fall, adv, out, cells, flow, inverse, ratio, level_out, staged,
    cell_sem, out_sem
):
    nx, ny, packed, _ = out.shape
    nz, bins = fall.shape
    halves = bins // LANES
    width, blocks = cells.shape
    slots = level_out.shape[0]

    fetch = pltpu.make_async_copy(spots, cells, cell_sem.at[0])
    fetch.start()
    inverse[...] = 1.0 / (1.0 + fall[...])
    ratio[...] = fall[...] * inverse[...]
    flow[...] = arrived[...].astype(F32)
    rim = edge_in[...].astype(F32)
    flow[0:ny, :] = rim[0:ny]
    flow[(nx - 1) * ny : nx * ny, :] = rim[ny : 2 * ny]
    for i in range(nx):
        flow[i * ny : i * ny + 1, :] = rim[2 * ny + i : 2 * ny + i + 1]
        flow[i * ny + ny - 1 : i * ny + ny, :] = rim[2 * ny + nx + i : 2 * ny + nx + i + 1]
    fetch.wait()

    def scatter(j, carry):
        for k in range(blocks):
            cell = pl.ds(cells[j, k], 1)
            for h in range(halves):
                adv[h, cell, :] = moist[h, pl.ds(j * blocks + k, 1), :]
        return carry

    lax.fori_loop(0, width, scatter, 0)

    def push(i):
        at = pl.ds(i * slots, slots)
        return pltpu.make_async_copy(staged.at[at], out.at[at], out_sem.at[i])

    def some_rows(i, carry):
        for slot in range(slots):
            x = i * slots + slot
            for g in range(ny // GROUP):
                column = pl.multiple_of(x * ny + g * GROUP, GROUP)
                for h in range(halves):
                    lanes = slice(h * LANES, (h + 1) * LANES)
                    inflow = flow[pl.ds(column, GROUP), lanes]
                    for z in reversed(range(nz)):
                        held = adv[h, pl.ds(pl.multiple_of(column * nz + z * GROUP, GROUP), GROUP), :] + inflow
                        to = pl.ds(g * GROUP * nz + z, GROUP, stride=nz)
                        level_out[slot, h, to, :] = held * inverse[z : z + 1, lanes]
                        inflow = held * ratio[z : z + 1, lanes]
            for y in range(ny):
                pieces = [level_out[slot, h, y * nz : (y + 1) * nz, :] for h in range(halves)]
                staged[x, y] = jnp.concatenate(pieces, axis=0).astype(BF16)
        push(i).start()
        return carry

    lax.fori_loop(0, nx // slots, some_rows, 0)
    for i in range(nx // slots):
        push(i).wait()


def body(
    spectrum,
    wind_east,
    wind_north,
    fall_rate,
    cloud_cells,
    block_target,
    pair_inputs,
    pair_outputs,
    loss_kernel,
    fragments,
):
    nx, ny, nz, bins = spectrum.shape
    halves = bins // LANES
    cells = nx * ny * nz
    columns = nx * ny
    blocks, width = cloud_cells.shape[3], cloud_cells.shape[4]
    total = blocks * width
    pairs = pair_outputs.shape[0]
    packed = nz * halves
    winds = (wind_east.transpose(0, 2, 1), wind_north.transpose(0, 2, 1))
    listed = cloud_cells.reshape(blocks, width).T
    dma = pltpu.SemaphoreType.DMA
    hbm = pl.BlockSpec(memory_space=pltpu.HBM)
    vmem = pl.BlockSpec(memory_space=pltpu.VMEM)
    dense = spectrum.reshape(nx, ny, nz, halves, LANES).transpose(0, 1, 3, 2, 4).reshape(nx, ny, packed, LANES)
    span = max(s for s in range(1, 11) if (nx - 2) % s == 0)
    inner = (nx - 2) // span
    rim = 2 * (nx + ny)
    parts = 4

    adv, moist, arrived, edge_in, spots, fall_v = pl.pallas_call(
        step_kernel,
        out_shape=(
            pltpu.VMEM((halves, cells, LANES), F32),
            pltpu.VMEM((halves, total, LANES), F32),
            pltpu.VMEM((columns, bins), BF16),
            pltpu.VMEM((rim, bins), BF16),
            pltpu.VMEM((width, blocks), I32),
            pltpu.VMEM(fall_rate.shape, F32),
        ),
        in_specs=[hbm] * 10,
        out_specs=(vmem,) * 6,
        scratch_shapes=[
            pltpu.VMEM((nx + 2, ny, packed, LANES), BF16),
            pltpu.VMEM(winds[0].shape, F32),
            pltpu.VMEM(winds[1].shape, F32),
            pltpu.VMEM((ny, packed, LANES), BF16),
            pltpu.VMEM((ny, packed, LANES), BF16),
            pltpu.VMEM((nx, packed, LANES), BF16),
            pltpu.VMEM((nx, packed, LANES), BF16),
            pltpu.SMEM((width, blocks), I32),
            pltpu.VMEM((width, blocks), I32),
            pltpu.VMEM(block_target.shape, I32),
            pltpu.VMEM(pair_inputs.shape, BF16),
            pltpu.VMEM(pair_outputs.shape, BF16),
            pltpu.VMEM(loss_kernel.shape, BF16),
            pltpu.VMEM(fragments.shape, BF16),
            pltpu.VMEM((halves, total, LANES), F32),
            pltpu.VMEM((total, bins), BF16),
            pltpu.VMEM((total, bins), F32),
            pltpu.VMEM((max(total // LANES, 8), LANES), I32),
            pltpu.VMEM((blocks, LANES), F32),
            pltpu.VMEM((2 * nz, bins), F32),
            pltpu.VMEM(((nx - 2) * ny, bins), F32),
            pltpu.VMEM(((nx - 2) * ny, bins), BF16),
            pltpu.VMEM((rim, bins), BF16),
            pltpu.VMEM((rim, bins), F32),
            dma((parts,)),
            dma((10,)),
            dma((1,)),
            dma((4,)),
            dma((4,)),
            dma((inner + 1,)),
            dma((inner + 1,)),
        ],
        compiler_params=pltpu.CompilerParams(
            collective_id=0, has_side_effects=True, vmem_limit_bytes=(60 << 20) - cells * bins * 4
        ),
        name="step",
    )(dense, *winds, fall_rate, listed, block_target, pair_inputs, pair_outputs, loss_kernel, fragments)

    slots = 4
    _, settled = pl.pallas_call(
        settle_kernel,
        out_shape=(
            pltpu.VMEM((halves, cells, LANES), F32),
            jax.ShapeDtypeStruct((nx, ny, packed, LANES), BF16),
        ),
        in_specs=[vmem] * 6,
        out_specs=(vmem, hbm),
        scratch_shapes=[
            pltpu.SMEM((width, blocks), I32),
            pltpu.VMEM((columns, bins), F32),
            pltpu.VMEM((nz, bins), F32),
            pltpu.VMEM((nz, bins), F32),
            pltpu.VMEM((slots, halves, ny * nz, LANES), F32),
            pltpu.VMEM((nx, ny, packed, LANES), BF16),
            dma((1,)),
            dma((nx // slots,)),
        ],
        input_output_aliases={0: 0},
        compiler_params=pltpu.CompilerParams(vmem_limit_bytes=32 << 20),
        name="settle",
    )(adv, moist, arrived, edge_in, spots, fall_v)
    return settled.reshape(nx, ny, halves, nz, LANES).transpose(0, 1, 3, 2, 4).reshape(nx, ny, nz, bins)


def solution(mesh):
    in_specs = (
        P("gx", "gy", "gz", None),
        P("gx", "gy", "gz"),
        P("gx", "gy", "gz"),
        P("gz", None),
        P("gx", "gy", "gz", None, None),
        P(None, None, "gz", None),
        P(),
        P(),
        P(),
        P(),
    )
    out_specs = P("gx", "gy", "gz", None)
    return jax.shard_map(body, mesh=mesh, in_specs=in_specs, out_specs=out_specs, check_vma=False)
```

```python
import functools

import jax
import jax.numpy as jnp
from jax import lax
from jax.experimental import pallas as pl
from jax.experimental.pallas import tpu as pltpu
from jax.sharding import PartitionSpec as P

MESH = pl.DeviceIdType.MESH
F32 = jnp.float32
BF16 = jnp.bfloat16
I32 = jnp.int32
LANES = 128
GROUP = 8


def spot_of(column, level, levels):
    return (column // GROUP * levels + level) * GROUP + column % GROUP


def step_kernel(
    spec, winds_e, winds_n, fall_h, cells_h, target_h, pair_in_h, pair_out_h, loss_h, frag_h,
    adv, moist, arrived, edge_in, spots, fall,
    local, we, wn, west, east, south, north, cells, listed_v, target, pair_in, pair_out, loss, frag,
    rows, q, pz, ids, live, shares, picks, table, settled, flux, edge_flux, extra,
    load_sem, in_sem, spot_sem, send_sem, recv_sem, down_sem, got_sem,
):
    nx, ny, packed, _ = spec.shape
    nz, bins = fall.shape
    halves = bins // LANES
    width, blocks = cells.shape
    total = width * blocks
    pairs = pair_out.shape[0]
    parts = load_sem.shape[0]
    per = nx // parts
    gx, gy, me = lax.axis_index("gx"), lax.axis_index("gy"), lax.axis_index("gz")
    sx, sy, count = lax.axis_size("gx"), lax.axis_size("gy"), lax.axis_size("gz")
    plane = sx * sy
    top = count - 1
    to_west = {"gx": lax.rem(gx + sx - 1, sx)}
    to_east = {"gx": lax.rem(gx + 1, sx)}
    to_south = {"gy": lax.rem(gy + sy - 1, sy)}
    to_north = {"gy": lax.rem(gy + 1, sy)}
    above = {"gz": lax.rem(me + 1, count)}
    below = {"gz": lax.rem(me + top, count)}

    barrier = pltpu.get_barrier_semaphore()
    for peer in (to_west, to_east, to_south, to_north, above, below):
        pl.semaphore_signal(barrier, inc=1, device_id=peer, device_id_type=MESH)

    def fetch(i, src, dst):
        return pltpu.make_async_copy(src, dst, in_sem.at[i])

    wind_loads = [fetch(0, winds_e, we), fetch(1, winds_n, wn)]
    loads = [
        pltpu.make_async_copy(spec.at[pl.ds(p * per, per)], local.at[pl.ds(1 + p * per, per)], load_sem.at[p])
        for p in range(parts)
    ]
    small = [fetch(2, fall_h, fall), fetch(3, cells_h, listed_v), fetch(4, target_h, target)]
    weights = [
        fetch(6, pair_in_h, pair_in), fetch(7, pair_out_h, pair_out), fetch(8, loss_h, loss), fetch(9, frag_h, frag)
    ]
    for load in small + wind_loads + loads + weights:
        load.start()
    pl.semaphore_wait(barrier, 6)

    sends = [
        pltpu.make_async_remote_copy(
            src_ref=src,
            dst_ref=dst,
            send_sem=send_sem.at[i],
            recv_sem=recv_sem.at[i],
            device_id=peer,
            device_id_type=MESH,
        )
        for i, (src, dst, peer) in enumerate(
            (
                (spec.at[:, ny - 1], south, to_north),
                (spec.at[:, 0], north, to_south),
                (spec.at[nx - 1], west, to_east),
                (spec.at[0], east, to_west),
            )
        )
    ]
    for send in sends:
        send.start()

    zero_row = jnp.zeros((ny, packed, LANES), BF16)
    local[0] = zero_row
    local[nx + 1] = zero_row

    def stacked(tile):
        return jnp.concatenate([tile] * halves, axis=0).astype(BF16)

    def spread(tile, y):
        return jnp.broadcast_to(tile[:, y : y + 1], (packed, LANES))

    def total_of(terms):
        while len(terms) > 1:
            terms = [a + b for a, b in zip(terms[::2], terms[1::2])]
        return terms[0]

    def sink(x):
        for g in range(ny // GROUP):
            at = pl.ds(pl.multiple_of(x * ny + g * GROUP, GROUP), GROUP)
            base = pl.multiple_of((x * ny + g * GROUP) * nz, GROUP * nz)
            for h in range(halves):
                lanes = slice(h * LANES, (h + 1) * LANES)
                terms = [adv[h, pl.ds(base + z * GROUP, GROUP), :] * shares[z : z + 1, lanes] for z in range(nz)]
                settled[at, lanes] = total_of(terms)

    share_rows = total // nx

    def two_rows(i, carry):
        for turn in range(2):
            one_row(2 * i + turn)
        return carry

    def one_row(x):
        both = jnp.concatenate([we[x]] * (halves // 2) + [wn[x]] * (halves // 2), axis=0).astype(BF16)
        some = pl.ds(pl.multiple_of(x * share_rows, share_rows), share_rows)
        pz[some, :] = jnp.dot(picks[some, :], table[...], preferred_element_type=F32)
        sink(jnp.maximum(x - 1, 0))

        zero = jnp.zeros((packed, LANES), BF16)
        behind = zero
        centre = local[x + 1, 0]
        for y in range(ny):
            ahead = local[x + 1, y + 1] if y + 1 < ny else zero
            pair = spread(both, y)
            a = jnp.concatenate([pair[0:nz]] * halves, axis=0)
            b = jnp.concatenate([pair[nz : 2 * nz]] * halves, axis=0)
            up_x = jnp.where(a > 0, local[x, y], local[x + 2, y])
            up_y = jnp.where(b > 0, behind, ahead)
            change = jnp.abs(a) * (up_x - centre) + jnp.abs(b) * (up_y - centre)
            value = centre.astype(F32) + change.astype(F32)
            base = pl.multiple_of((x * ny + y - y % GROUP) * nz, GROUP * nz)
            for h in range(halves):
                adv[h, pl.ds(base + y % GROUP, nz, stride=GROUP), :] = value[h * nz : (h + 1) * nz]
            behind, centre = centre, ahead

    for load in small:
        load.wait()

    ratio = fall[...] / (1.0 + fall[...])
    share = jnp.ones((1, bins), F32)
    for z in range(nz):
        share = share * ratio[z : z + 1, :]
        shares[z : z + 1, :] = share
    shares[nz : 2 * nz, :] = ratio
    gain = share

    listed = listed_v[...]
    spots[...] = spot_of(listed // nz, listed % nz, nz)
    spot = pltpu.make_async_copy(spots, cells, spot_sem.at[0])
    spot.start()
    cloudy = target[gx, gy] < plane
    columns = jnp.where(cloudy, listed // nz, -1)
    per_tile = LANES // blocks
    for t in range(total // LANES):
        ids[t : t + 1, :] = jnp.concatenate(
            [columns[t * per_tile + i : t * per_tile + i + 1, :] for i in range(per_tile)], axis=1
        )
    flags = jnp.broadcast_to(jnp.where(cloudy, 1.0, 0.0), (8, blocks)).T
    live[...] = jnp.broadcast_to(flags[:, 0:1], (blocks, LANES))
    heights = (listed % nz).astype(F32).T
    high = shares[0:nz, :].astype(BF16)
    low = (shares[0:nz, :] - high.astype(F32)).astype(BF16)
    table[...] = jnp.concatenate([high, low, jnp.zeros((LANES - 2 * nz, bins), BF16)], axis=0)
    lane = lax.broadcasted_iota(I32, (blocks, LANES), 1)
    level_of = jnp.where(lane < 2 * nz, lane % nz, -1).astype(F32)
    for j in range(width):
        hit = jnp.broadcast_to(heights[:, j : j + 1], (blocks, LANES)) == level_of
        picks[j * blocks : (j + 1) * blocks, :] = jnp.where(hit, 1.0, 0.0).astype(BF16)

    for load in wind_loads:
        load.wait()
    done = 0
    for p in range(parts):
        loads[p].wait()
        upto = nx // 2 if p == parts - 1 else ((p + 1) * per - 1) // 2
        lax.fori_loop(done, upto, two_rows, 0)
        done = upto

    for load in weights:
        load.wait()

    size = min(512, total)
    tile = min(256, pairs)
    inner = down_sem.shape[0] - 1
    span = (nx - 2) // inner
    wide = span * ny

    def gather(i):
        for r in range(i * size, (i + 1) * size):
            cell = pl.ds(cells[r // blocks, r % blocks], 1)
            for h in range(halves):
                rows[h, r : r + 1, :] = adv[h, cell, :]

    def collide(i):
        at = slice(i * size, (i + 1) * size)
        full = jnp.concatenate([rows[h, at, :] for h in range(halves)], axis=1)
        row = full.astype(BF16)
        decline = jnp.dot(row, loss[...], preferred_element_type=F32)
        losses = row.astype(F32) * decline
        gained = jnp.dot(losses.astype(BF16), frag[...], preferred_element_type=F32)
        for n in range(0, pairs, tile):
            first = jnp.dot(row, pair_in[:, n : n + tile], preferred_element_type=F32)
            second = jnp.dot(row, pair_in[:, pairs + n : pairs + n + tile], preferred_element_type=F32)
            product = (first * second).astype(BF16)
            gained = gained + jnp.dot(product, pair_out[n : n + tile, :], preferred_element_type=F32)
        tendency = (gained - losses).astype(BF16).astype(F32)
        alive = jnp.concatenate([jnp.concatenate([live[...]] * halves, axis=1)] * (size // blocks), axis=0)
        tendency = jnp.where(alive > 0.0, tendency, 0.0)
        q[at, :] = (tendency * pz[at, :]).astype(BF16)
        after = full + tendency
        for h in range(halves):
            moist[h, at, :] = after[:, h * LANES : (h + 1) * LANES]

    def collide_all():
        chunks = total // size
        gather(0)
        for i in range(chunks):
            if i + 1 < chunks:
                gather(i + 1)
            collide(i)

    def collected(column):
        hot = [
            jnp.where(jnp.broadcast_to(ids[t : t + 1, :], column.shape) == column, 1.0, 0.0).astype(BF16)
            for t in range(total // LANES)
        ]
        return jnp.dot(jnp.concatenate(hot, axis=1), q[...], preferred_element_type=F32)

    def drained(column, apart, lanes, h):
        first = spot_of(column, 0, nz)
        stride = 1 if apart == 1 else apart * nz
        terms = [
            adv[h, pl.ds(first + z * GROUP, GROUP, stride=stride), :] * shares[z : z + 1, lanes] for z in range(nz)
        ]
        return total_of(terms)

    def down(p):
        src = edge_flux if p == inner else flux.at[pl.ds(p * wide, wide)]
        dst = edge_in if p == inner else arrived.at[pl.ds((1 + p * span) * ny, wide)]
        return pltpu.make_async_remote_copy(
            src_ref=src,
            dst_ref=dst,
            send_sem=down_sem.at[p],
            recv_sem=got_sem.at[p],
            device_id={"gz": jnp.maximum(me - 1, 0)},
            device_id_type=MESH,
        )

    def relay(p):
        down(p).wait_recv()

        @pl.when(me > 0)
        def _():
            if p == inner:
                edge_flux[...] = (edge_flux[...].astype(F32) + edge_in[...].astype(F32) * gain).astype(BF16)
            else:
                at = pl.ds(p * wide, wide)
                got = arrived[pl.ds((1 + p * span) * ny, wide), :].astype(F32)
                flux[at, :] = (flux[at, :].astype(F32) + got * gain).astype(BF16)
            down(p).start()

    spot.wait()
    collide_all()

    for p in range(inner):
        column = lax.broadcasted_iota(I32, (wide, LANES), 0) + (1 + p * span) * ny
        held = settled[(1 + p * span) * ny : (1 + (p + 1) * span) * ny, :]
        flux[p * wide : (p + 1) * wide, :] = (collected(column) + held).astype(BF16)

    for p in range(inner):

        @pl.when(me == top)
        def _():
            down(p).start()

        @pl.when(me == top - 1)
        def _():
            relay(p)

    for send in sends[:2]:
        send.wait_recv()

    def add_halo(column, wind, halo):
        came = wind.astype(F32) * halo.astype(F32)
        at = pl.ds(spot_of(column, 0, nz), nz, stride=GROUP)
        for h in range(halves):
            adv[h, at, :] = adv[h, at, :] + came[h * nz : (h + 1) * nz]

    def edges(x, carry):
        winds = stacked(wn[x])
        add_halo(x * ny, jnp.maximum(spread(winds, 0), 0), south[x])
        add_halo(x * ny + ny - 1, jnp.maximum(-spread(winds, ny - 1), 0), north[x])
        return carry

    lax.fori_loop(0, nx, edges, 0, unroll=8)

    for send, x, halo, sign in ((sends[2], 0, west, 1.0), (sends[3], nx - 1, east, -1.0)):
        send.wait_recv()
        winds = jnp.maximum(sign * stacked(we[x]), 0)
        for y in range(ny):
            add_halo(x * ny + y, spread(winds, y), halo[y])

    collide_all()

    rim = edge_flux.shape[0]
    order = lax.broadcasted_iota(I32, (rim, LANES), 0)
    near = jnp.where(order < ny, order, order - ny + (nx - 1) * ny)
    far = order - 2 * ny
    side = jnp.where(far < nx, far * ny, (far - nx) * ny + ny - 1)
    extra[0:rim, :] = collected(jnp.where(order < 2 * ny, near, side))
    for r in range(0, rim, GROUP):
        if r < 2 * ny:
            x, y = (0, r) if r < ny else (nx - 1, r - ny)
            base, stride = x * ny + y, 1
        else:
            x, y = (r - 2 * ny, 0) if r - 2 * ny < nx else (r - 2 * ny - nx, ny - 1)
            base, stride = x * ny + y, ny
        for h in range(halves):
            lanes = slice(h * LANES, (h + 1) * LANES)
            extra[r : r + GROUP, lanes] = extra[r : r + GROUP, lanes] + drained(base, stride, lanes, h)
    edge_flux[...] = extra[0:rim, :].astype(BF16)

    @pl.when(me == top)
    def _():
        down(inner).start()
        arrived[...] = jnp.zeros(arrived.shape, BF16)
        edge_in[...] = jnp.zeros(edge_in.shape, BF16)

    @pl.when(me == top - 1)
    def _():
        relay(inner)

    @pl.when(me < top - 1)
    def _():
        for p in range(inner + 1):
            relay(p)

    @pl.when(me > 0)
    def _():
        for p in range(inner + 1):
            down(p).wait_send()

    for send in sends:
        send.wait_send()


def settle_kernel(
    adv_in, moist, arrived, edge_in, spots, fall, adv, out, cells, flow, inverse, ratio, level_out, staged,
    cell_sem, out_sem
):
    nx, ny, packed, _ = out.shape
    nz, bins = fall.shape
    halves = bins // LANES
    width, blocks = cells.shape
    slots = level_out.shape[0]

    fetch = pltpu.make_async_copy(spots, cells, cell_sem.at[0])
    fetch.start()
    inverse[...] = 1.0 / (1.0 + fall[...])
    ratio[...] = fall[...] * inverse[...]
    flow[...] = arrived[...].astype(F32)
    rim = edge_in[...].astype(F32)
    flow[0:ny, :] = rim[0:ny]
    flow[(nx - 1) * ny : nx * ny, :] = rim[ny : 2 * ny]
    for i in range(nx):
        flow[i * ny : i * ny + 1, :] = rim[2 * ny + i : 2 * ny + i + 1]
        flow[i * ny + ny - 1 : i * ny + ny, :] = rim[2 * ny + nx + i : 2 * ny + nx + i + 1]
    fetch.wait()

    for r in range(width * blocks):
        cell = pl.ds(cells[r // blocks, r % blocks], 1)
        for h in range(halves):
            adv[h, cell, :] = moist[h, r : r + 1, :]

    def push(i):
        at = pl.ds(i * slots, slots)
        return pltpu.make_async_copy(staged.at[at], out.at[at], out_sem.at[i])

    def some_rows(i, carry):
        for slot in range(slots):
            x = i * slots + slot
            for g in range(ny // GROUP):
                column = pl.multiple_of(x * ny + g * GROUP, GROUP)
                for h in range(halves):
                    lanes = slice(h * LANES, (h + 1) * LANES)
                    inflow = flow[pl.ds(column, GROUP), lanes]
                    for z in reversed(range(nz)):
                        held = adv[h, pl.ds(pl.multiple_of(column * nz + z * GROUP, GROUP), GROUP), :] + inflow
                        to = pl.ds(g * GROUP * nz + z, GROUP, stride=nz)
                        level_out[slot, h, to, :] = held * inverse[z : z + 1, lanes]
                        inflow = held * ratio[z : z + 1, lanes]
            for y in range(ny):
                pieces = [level_out[slot, h, y * nz : (y + 1) * nz, :] for h in range(halves)]
                staged[x, y] = jnp.concatenate(pieces, axis=0).astype(BF16)
        push(i).start()
        return carry

    lax.fori_loop(0, nx // slots, some_rows, 0)
    for i in range(nx // slots):
        push(i).wait()


def body(
    spectrum,
    wind_east,
    wind_north,
    fall_rate,
    cloud_cells,
    block_target,
    pair_inputs,
    pair_outputs,
    loss_kernel,
    fragments,
):
    nx, ny, nz, bins = spectrum.shape
    halves = bins // LANES
    cells = nx * ny * nz
    columns = nx * ny
    blocks, width = cloud_cells.shape[3], cloud_cells.shape[4]
    total = blocks * width
    pairs = pair_outputs.shape[0]
    packed = nz * halves
    winds = (wind_east.transpose(0, 2, 1), wind_north.transpose(0, 2, 1))
    listed = cloud_cells.reshape(blocks, width).T
    dma = pltpu.SemaphoreType.DMA
    hbm = pl.BlockSpec(memory_space=pltpu.HBM)
    vmem = pl.BlockSpec(memory_space=pltpu.VMEM)
    dense = spectrum.reshape(nx, ny, nz, halves, LANES).transpose(0, 1, 3, 2, 4).reshape(nx, ny, packed, LANES)
    span = max(s for s in range(1, 11) if (nx - 2) % s == 0)
    inner = (nx - 2) // span
    rim = 2 * (nx + ny)
    parts = 4

    adv, moist, arrived, edge_in, spots, fall_v = pl.pallas_call(
        step_kernel,
        out_shape=(
            pltpu.VMEM((halves, cells, LANES), F32),
            pltpu.VMEM((halves, total, LANES), F32),
            pltpu.VMEM((columns, bins), BF16),
            pltpu.VMEM((rim, bins), BF16),
            pltpu.VMEM((width, blocks), I32),
            pltpu.VMEM(fall_rate.shape, F32),
        ),
        in_specs=[hbm] * 10,
        out_specs=(vmem,) * 6,
        scratch_shapes=[
            pltpu.VMEM((nx + 2, ny, packed, LANES), BF16),
            pltpu.VMEM(winds[0].shape, F32),
            pltpu.VMEM(winds[1].shape, F32),
            pltpu.VMEM((ny, packed, LANES), BF16),
            pltpu.VMEM((ny, packed, LANES), BF16),
            pltpu.VMEM((nx, packed, LANES), BF16),
            pltpu.VMEM((nx, packed, LANES), BF16),
            pltpu.SMEM((width, blocks), I32),
            pltpu.VMEM((width, blocks), I32),
            pltpu.VMEM(block_target.shape, I32),
            pltpu.VMEM(pair_inputs.shape, BF16),
            pltpu.VMEM(pair_outputs.shape, BF16),
            pltpu.VMEM(loss_kernel.shape, BF16),
            pltpu.VMEM(fragments.shape, BF16),
            pltpu.VMEM((halves, total, LANES), F32),
            pltpu.VMEM((total, bins), BF16),
            pltpu.VMEM((total, bins), F32),
            pltpu.VMEM((max(total // LANES, 8), LANES), I32),
            pltpu.VMEM((blocks, LANES), F32),
            pltpu.VMEM((2 * nz, bins), F32),
            pltpu.VMEM((total, LANES), BF16),
            pltpu.VMEM((LANES, bins), BF16),
            pltpu.VMEM((columns, bins), F32),
            pltpu.VMEM(((nx - 2) * ny, bins), BF16),
            pltpu.VMEM((rim, bins), BF16),
            pltpu.VMEM((rim, bins), F32),
            dma((parts,)),
            dma((10,)),
            dma((1,)),
            dma((4,)),
            dma((4,)),
            dma((inner + 1,)),
            dma((inner + 1,)),
        ],
        compiler_params=pltpu.CompilerParams(
            collective_id=0, has_side_effects=True, vmem_limit_bytes=(60 << 20) - cells * bins * 4
        ),
        name="step",
    )(dense, *winds, fall_rate, listed, block_target, pair_inputs, pair_outputs, loss_kernel, fragments)

    slots = 8
    _, settled = pl.pallas_call(
        settle_kernel,
        out_shape=(
            pltpu.VMEM((halves, cells, LANES), F32),
            jax.ShapeDtypeStruct((nx, ny, packed, LANES), BF16),
        ),
        in_specs=[vmem] * 6,
        out_specs=(vmem, hbm),
        scratch_shapes=[
            pltpu.SMEM((width, blocks), I32),
            pltpu.VMEM((columns, bins), F32),
            pltpu.VMEM((nz, bins), F32),
            pltpu.VMEM((nz, bins), F32),
            pltpu.VMEM((slots, halves, ny * nz, LANES), F32),
            pltpu.VMEM((nx, ny, packed, LANES), BF16),
            dma((1,)),
            dma((nx // slots,)),
        ],
        input_output_aliases={0: 0},
        compiler_params=pltpu.CompilerParams(vmem_limit_bytes=32 << 20),
        name="settle",
    )(adv, moist, arrived, edge_in, spots, fall_v)
    return settled.reshape(nx, ny, halves, nz, LANES).transpose(0, 1, 3, 2, 4).reshape(nx, ny, nz, bins)


def solution(mesh):
    in_specs = (
        P("gx", "gy", "gz", None),
        P("gx", "gy", "gz"),
        P("gx", "gy", "gz"),
        P("gz", None),
        P("gx", "gy", "gz", None, None),
        P(None, None, "gz", None),
        P(),
        P(),
        P(),
        P(),
    )
    out_specs = P("gx", "gy", "gz", None)
    return jax.shard_map(body, mesh=mesh, in_specs=in_specs, out_specs=out_specs, check_vma=False)
```

```python
import functools

import jax
import jax.numpy as jnp
from jax import lax
from jax.experimental import pallas as pl
from jax.experimental.pallas import tpu as pltpu
from jax.sharding import PartitionSpec as P

MESH = pl.DeviceIdType.MESH
F32 = jnp.float32
BF16 = jnp.bfloat16
I32 = jnp.int32
LANES = 128
GROUP = 8


def spot_of(column, level, levels):
    return (column // GROUP * levels + level) * GROUP + column % GROUP


def step_kernel(
    spec, winds_e, winds_n, fall_h, cells_h, target_h, pair_in_h, pair_out_h, loss_h, frag_h,
    adv, moist, arrived, edge_in, spots, fall,
    local, we, wn, west, east, south, north, cells, listed_v, target, pair_in, pair_out, loss, frag,
    rows, q, pz, ids, live, shares, picks, table, settled, flux, edge_flux, extra,
    load_sem, in_sem, spot_sem, send_sem, recv_sem, down_sem, got_sem,
):
    nx, ny, packed, _ = spec.shape
    nz, bins = fall.shape
    halves = bins // LANES
    width, blocks = cells.shape
    total = width * blocks
    pairs = pair_out.shape[0]
    parts = load_sem.shape[0]
    per = nx // parts
    gx, gy, me = lax.axis_index("gx"), lax.axis_index("gy"), lax.axis_index("gz")
    sx, sy, count = lax.axis_size("gx"), lax.axis_size("gy"), lax.axis_size("gz")
    plane = sx * sy
    top = count - 1
    to_west = {"gx": lax.rem(gx + sx - 1, sx)}
    to_east = {"gx": lax.rem(gx + 1, sx)}
    to_south = {"gy": lax.rem(gy + sy - 1, sy)}
    to_north = {"gy": lax.rem(gy + 1, sy)}
    above = {"gz": lax.rem(me + 1, count)}
    below = {"gz": lax.rem(me + top, count)}

    barrier = pltpu.get_barrier_semaphore()
    for peer in (to_west, to_east, to_south, to_north, above, below):
        pl.semaphore_signal(barrier, inc=1, device_id=peer, device_id_type=MESH)

    def fetch(i, src, dst):
        return pltpu.make_async_copy(src, dst, in_sem.at[i])

    wind_loads = [fetch(0, winds_e, we), fetch(1, winds_n, wn)]
    loads = [
        pltpu.make_async_copy(spec.at[pl.ds(p * per, per)], local.at[pl.ds(1 + p * per, per)], load_sem.at[p])
        for p in range(parts)
    ]
    small = [fetch(2, fall_h, fall), fetch(3, cells_h, listed_v), fetch(4, target_h, target)]
    weights = [
        fetch(6, pair_in_h, pair_in), fetch(7, pair_out_h, pair_out), fetch(8, loss_h, loss), fetch(9, frag_h, frag)
    ]
    for load in small + wind_loads + loads + weights:
        load.start()
    pl.semaphore_wait(barrier, 6)

    sends = [
        pltpu.make_async_remote_copy(
            src_ref=src,
            dst_ref=dst,
            send_sem=send_sem.at[i],
            recv_sem=recv_sem.at[i],
            device_id=peer,
            device_id_type=MESH,
        )
        for i, (src, dst, peer) in enumerate(
            (
                (spec.at[:, ny - 1], south, to_north),
                (spec.at[:, 0], north, to_south),
                (spec.at[nx - 1], west, to_east),
                (spec.at[0], east, to_west),
            )
        )
    ]
    for send in sends:
        send.start()

    zero_row = jnp.zeros((ny, packed, LANES), BF16)
    local[0] = zero_row
    local[nx + 1] = zero_row

    def stacked(tile):
        return jnp.concatenate([tile] * halves, axis=0).astype(BF16)

    def spread(tile, y):
        return jnp.broadcast_to(tile[:, y : y + 1], (packed, LANES))

    def total_of(terms):
        while len(terms) > 1:
            terms = [a + b for a, b in zip(terms[::2], terms[1::2])]
        return terms[0]

    def sink(x):
        for g in range(ny // GROUP):
            at = pl.ds(pl.multiple_of(x * ny + g * GROUP, GROUP), GROUP)
            base = pl.multiple_of((x * ny + g * GROUP) * nz, GROUP * nz)
            for h in range(halves):
                lanes = slice(h * LANES, (h + 1) * LANES)
                terms = [adv[h, pl.ds(base + z * GROUP, GROUP), :] * shares[z : z + 1, lanes] for z in range(nz)]
                settled[at, lanes] = total_of(terms)

    share_rows = total // nx

    def two_rows(i, carry):
        for turn in range(2):
            one_row(2 * i + turn)
        return carry

    def one_row(x):
        both = jnp.concatenate([we[x]] * (halves // 2) + [wn[x]] * (halves // 2), axis=0).astype(BF16)
        some = pl.ds(pl.multiple_of(x * share_rows, share_rows), share_rows)
        pz[some, :] = jnp.dot(picks[some, :], table[...], preferred_element_type=F32)
        sink(jnp.maximum(x - 1, 0))

        zero = jnp.zeros((packed, LANES), BF16)
        behind = zero
        centre = local[x + 1, 0]
        for y in range(ny):
            ahead = local[x + 1, y + 1] if y + 1 < ny else zero
            pair = spread(both, y)
            a = jnp.concatenate([pair[0:nz]] * halves, axis=0)
            b = jnp.concatenate([pair[nz : 2 * nz]] * halves, axis=0)
            up_x = jnp.where(a > 0, local[x, y], local[x + 2, y])
            up_y = jnp.where(b > 0, behind, ahead)
            change = jnp.abs(a) * (up_x - centre) + jnp.abs(b) * (up_y - centre)
            value = centre.astype(F32) + change.astype(F32)
            base = pl.multiple_of((x * ny + y - y % GROUP) * nz, GROUP * nz)
            for h in range(halves):
                adv[h, pl.ds(base + y % GROUP, nz, stride=GROUP), :] = value[h * nz : (h + 1) * nz]
            behind, centre = centre, ahead

    for load in small:
        load.wait()

    ratio = fall[...] / (1.0 + fall[...])
    share = jnp.ones((1, bins), F32)
    for z in range(nz):
        share = share * ratio[z : z + 1, :]
        shares[z : z + 1, :] = share
    shares[nz : 2 * nz, :] = ratio
    gain = share

    listed = listed_v[...]
    spots[...] = spot_of(listed // nz, listed % nz, nz)
    spot = pltpu.make_async_copy(spots, cells, spot_sem.at[0])
    spot.start()
    cloudy = target[gx, gy] < plane
    columns = jnp.where(cloudy, listed // nz, -1)
    per_tile = LANES // blocks
    for t in range(total // LANES):
        ids[t : t + 1, :] = jnp.concatenate(
            [columns[t * per_tile + i : t * per_tile + i + 1, :] for i in range(per_tile)], axis=1
        )
    flags = jnp.broadcast_to(jnp.where(cloudy, 1.0, 0.0), (8, blocks)).T
    live[...] = jnp.broadcast_to(flags[:, 0:1], (blocks, LANES))
    heights = (listed % nz).astype(F32).T
    high = shares[0:nz, :].astype(BF16)
    low = (shares[0:nz, :] - high.astype(F32)).astype(BF16)
    table[...] = jnp.concatenate([high, low, jnp.zeros((LANES - 2 * nz, bins), BF16)], axis=0)
    lane = lax.broadcasted_iota(I32, (blocks, LANES), 1)
    level_of = jnp.where(lane < 2 * nz, lane % nz, -1).astype(F32)
    for j in range(width):
        hit = jnp.broadcast_to(heights[:, j : j + 1], (blocks, LANES)) == level_of
        picks[j * blocks : (j + 1) * blocks, :] = jnp.where(hit, 1.0, 0.0).astype(BF16)

    for load in wind_loads:
        load.wait()
    done = 0
    for p in range(parts):
        loads[p].wait()
        upto = nx // 2 if p == parts - 1 else ((p + 1) * per - 1) // 2
        lax.fori_loop(done, upto, two_rows, 0)
        done = upto

    for load in weights:
        load.wait()

    size = min(512, total)
    tile = min(256, pairs)
    inner = down_sem.shape[0] - 2
    span = (nx - 2) // inner
    wide = span * ny

    def gather(i):
        for r in range(i * size, (i + 1) * size):
            cell = pl.ds(cells[r // blocks, r % blocks], 1)
            for h in range(halves):
                rows[h, r : r + 1, :] = adv[h, cell, :]

    def collide(i):
        at = slice(i * size, (i + 1) * size)
        full = jnp.concatenate([rows[h, at, :] for h in range(halves)], axis=1)
        row = full.astype(BF16)
        decline = jnp.dot(row, loss[...], preferred_element_type=F32)
        losses = row.astype(F32) * decline
        gained = jnp.dot(losses.astype(BF16), frag[...], preferred_element_type=F32)
        for n in range(0, pairs, tile):
            first = jnp.dot(row, pair_in[:, n : n + tile], preferred_element_type=F32)
            second = jnp.dot(row, pair_in[:, pairs + n : pairs + n + tile], preferred_element_type=F32)
            product = (first * second).astype(BF16)
            gained = gained + jnp.dot(product, pair_out[n : n + tile, :], preferred_element_type=F32)
        tendency = (gained - losses).astype(BF16).astype(F32)
        alive = jnp.concatenate([jnp.concatenate([live[...]] * halves, axis=1)] * (size // blocks), axis=0)
        tendency = jnp.where(alive > 0.0, tendency, 0.0)
        q[at, :] = (tendency * pz[at, :]).astype(BF16)
        after = full + tendency
        for h in range(halves):
            moist[h, at, :] = after[:, h * LANES : (h + 1) * LANES]

    def collide_all():
        chunks = total // size
        gather(0)
        for i in range(chunks):
            if i + 1 < chunks:
                gather(i + 1)
            collide(i)

    def collected(column):
        hot = [
            jnp.where(jnp.broadcast_to(ids[t : t + 1, :], column.shape) == column, 1.0, 0.0).astype(BF16)
            for t in range(total // LANES)
        ]
        return jnp.dot(jnp.concatenate(hot, axis=1), q[...], preferred_element_type=F32)

    def drained(column, apart, lanes, h):
        first = spot_of(column, 0, nz)
        stride = 1 if apart == 1 else apart * nz
        terms = [
            adv[h, pl.ds(first + z * GROUP, GROUP, stride=stride), :] * shares[z : z + 1, lanes] for z in range(nz)
        ]
        return total_of(terms)

    edge = {inner: slice(0, 2 * ny), inner + 1: slice(2 * ny, 2 * (ny + nx))}

    def down(p):
        src = edge_flux.at[edge[p]] if p in edge else flux.at[pl.ds(p * wide, wide)]
        dst = edge_in.at[edge[p]] if p in edge else arrived.at[pl.ds((1 + p * span) * ny, wide)]
        return pltpu.make_async_remote_copy(
            src_ref=src,
            dst_ref=dst,
            send_sem=down_sem.at[p],
            recv_sem=got_sem.at[p],
            device_id={"gz": jnp.maximum(me - 1, 0)},
            device_id_type=MESH,
        )

    def relay(p):
        down(p).wait_recv()

        @pl.when(me > 0)
        def _():
            if p in edge:
                at = edge[p]
                edge_flux[at, :] = (edge_flux[at, :].astype(F32) + edge_in[at, :].astype(F32) * gain).astype(BF16)
            else:
                at = pl.ds(p * wide, wide)
                got = arrived[pl.ds((1 + p * span) * ny, wide), :].astype(F32)
                flux[at, :] = (flux[at, :].astype(F32) + got * gain).astype(BF16)
            down(p).start()

    spot.wait()
    collide_all()

    for p in range(inner):
        half = wide // 2
        for part in range(2):
            start = p * wide + part * half
            column = lax.broadcasted_iota(I32, (half, LANES), 0) + (ny + start)
            held = settled[ny + start : ny + start + half, :]
            flux[start : start + half, :] = (collected(column) + held).astype(BF16)

        @pl.when(me == top)
        def _():
            down(p).start()

        @pl.when(me == top - 1)
        def _():
            relay(p)

    for send in sends[:2]:
        send.wait_recv()

    def add_halo(column, wind, halo):
        came = wind.astype(F32) * halo.astype(F32)
        at = pl.ds(spot_of(column, 0, nz), nz, stride=GROUP)
        for h in range(halves):
            adv[h, at, :] = adv[h, at, :] + came[h * nz : (h + 1) * nz]

    def edges(x, carry):
        winds = stacked(wn[x])
        add_halo(x * ny, jnp.maximum(spread(winds, 0), 0), south[x])
        add_halo(x * ny + ny - 1, jnp.maximum(-spread(winds, ny - 1), 0), north[x])
        return carry

    lax.fori_loop(0, nx, edges, 0, unroll=8)

    for send, x, halo, sign in ((sends[2], 0, west, 1.0), (sends[3], nx - 1, east, -1.0)):
        send.wait_recv()
        winds = jnp.maximum(sign * stacked(we[x]), 0)
        for y in range(ny):
            add_halo(x * ny + y, spread(winds, y), halo[y])

    collide_all()

    for p, at in edge.items():
        order = lax.broadcasted_iota(I32, (at.stop - at.start, LANES), 0)
        if p == inner:
            column = jnp.where(order < ny, order, order - ny + (nx - 1) * ny)
        else:
            column = jnp.where(order < nx, order * ny, (order - nx) * ny + ny - 1)
        extra[at, :] = collected(column)
        for r in range(at.start, at.stop, GROUP):
            if p == inner:
                first, apart = (r, 1) if r < ny else (r - ny + (nx - 1) * ny, 1)
            else:
                i = r - 2 * ny
                first, apart = (i * ny, ny) if i < nx else ((i - nx) * ny + ny - 1, ny)
            for h in range(halves):
                lanes = slice(h * LANES, (h + 1) * LANES)
                extra[r : r + GROUP, lanes] = extra[r : r + GROUP, lanes] + drained(first, apart, lanes, h)
        edge_flux[at, :] = extra[at, :].astype(BF16)

        @pl.when(me == top)
        def _():
            down(p).start()

    @pl.when(me == top)
    def _():
        arrived[...] = jnp.zeros(arrived.shape, BF16)
        edge_in[...] = jnp.zeros(edge_in.shape, BF16)

    @pl.when(me == top - 1)
    def _():
        for p in edge:
            relay(p)

    @pl.when(me < top - 1)
    def _():
        for p in range(inner + 2):
            relay(p)

    @pl.when(me > 0)
    def _():
        for p in range(inner + 2):
            down(p).wait_send()

    for send in sends:
        send.wait_send()


def settle_kernel(
    adv_in, moist, arrived, edge_in, spots, fall, adv, out, cells, flow, inverse, ratio, level_out, staged,
    cell_sem, out_sem
):
    nx, ny, packed, _ = out.shape
    nz, bins = fall.shape
    halves = bins // LANES
    width, blocks = cells.shape
    slots = level_out.shape[0]
    each = nx // out_sem.shape[0]

    fetch = pltpu.make_async_copy(spots, cells, cell_sem.at[0])
    fetch.start()
    inverse[...] = 1.0 / (1.0 + fall[...])
    ratio[...] = fall[...] * inverse[...]
    flow[...] = arrived[...].astype(F32)
    rim = edge_in[...].astype(F32)
    flow[0:ny, :] = rim[0:ny]
    flow[(nx - 1) * ny : nx * ny, :] = rim[ny : 2 * ny]
    for i in range(nx):
        flow[i * ny : i * ny + 1, :] = rim[2 * ny + i : 2 * ny + i + 1]
        flow[i * ny + ny - 1 : i * ny + ny, :] = rim[2 * ny + nx + i : 2 * ny + nx + i + 1]
    fetch.wait()

    for r in range(width * blocks):
        cell = pl.ds(cells[r // blocks, r % blocks], 1)
        for h in range(halves):
            adv[h, cell, :] = moist[h, r : r + 1, :]

    def push(i):
        at = pl.ds(i * each, each)
        return pltpu.make_async_copy(staged.at[at], out.at[at], out_sem.at[i])

    def some_rows(i, carry):
        for slot in range(slots):
            x = i * slots + slot
            for g in range(ny // GROUP):
                column = pl.multiple_of(x * ny + g * GROUP, GROUP)
                for h in range(halves):
                    lanes = slice(h * LANES, (h + 1) * LANES)
                    inflow = flow[pl.ds(column, GROUP), lanes]
                    for z in reversed(range(nz)):
                        held = adv[h, pl.ds(pl.multiple_of(column * nz + z * GROUP, GROUP), GROUP), :] + inflow
                        to = pl.ds(g * GROUP * nz + z, GROUP, stride=nz)
                        level_out[slot, h, to, :] = held * inverse[z : z + 1, lanes]
                        inflow = held * ratio[z : z + 1, lanes]
            for y in range(ny):
                pieces = [level_out[slot, h, y * nz : (y + 1) * nz, :] for h in range(halves)]
                staged[x, y] = jnp.concatenate(pieces, axis=0).astype(BF16)
            if (slot + 1) % each == 0:
                push((x + 1) // each - 1).start()
        return carry

    lax.fori_loop(0, nx // slots, some_rows, 0)
    for i in range(nx // each):
        push(i).wait()


def body(
    spectrum,
    wind_east,
    wind_north,
    fall_rate,
    cloud_cells,
    block_target,
    pair_inputs,
    pair_outputs,
    loss_kernel,
    fragments,
):
    nx, ny, nz, bins = spectrum.shape
    halves = bins // LANES
    cells = nx * ny * nz
    columns = nx * ny
    blocks, width = cloud_cells.shape[3], cloud_cells.shape[4]
    total = blocks * width
    pairs = pair_outputs.shape[0]
    packed = nz * halves
    winds = (wind_east.transpose(0, 2, 1), wind_north.transpose(0, 2, 1))
    listed = cloud_cells.reshape(blocks, width).T
    dma = pltpu.SemaphoreType.DMA
    hbm = pl.BlockSpec(memory_space=pltpu.HBM)
    vmem = pl.BlockSpec(memory_space=pltpu.VMEM)
    dense = spectrum.reshape(nx, ny, nz, halves, LANES).transpose(0, 1, 3, 2, 4).reshape(nx, ny, packed, LANES)
    span = max(s for s in range(1, 7) if (nx - 2) % s == 0)
    inner = (nx - 2) // span
    rim = 2 * (nx + ny)
    parts = 4

    adv, moist, arrived, edge_in, spots, fall_v = pl.pallas_call(
        step_kernel,
        out_shape=(
            pltpu.VMEM((halves, cells, LANES), F32),
            pltpu.VMEM((halves, total, LANES), F32),
            pltpu.VMEM((columns, bins), BF16),
            pltpu.VMEM((rim, bins), BF16),
            pltpu.VMEM((width, blocks), I32),
            pltpu.VMEM(fall_rate.shape, F32),
        ),
        in_specs=[hbm] * 10,
        out_specs=(vmem,) * 6,
        scratch_shapes=[
            pltpu.VMEM((nx + 2, ny, packed, LANES), BF16),
            pltpu.VMEM(winds[0].shape, F32),
            pltpu.VMEM(winds[1].shape, F32),
            pltpu.VMEM((ny, packed, LANES), BF16),
            pltpu.VMEM((ny, packed, LANES), BF16),
            pltpu.VMEM((nx, packed, LANES), BF16),
            pltpu.VMEM((nx, packed, LANES), BF16),
            pltpu.SMEM((width, blocks), I32),
            pltpu.VMEM((width, blocks), I32),
            pltpu.VMEM(block_target.shape, I32),
            pltpu.VMEM(pair_inputs.shape, BF16),
            pltpu.VMEM(pair_outputs.shape, BF16),
            pltpu.VMEM(loss_kernel.shape, BF16),
            pltpu.VMEM(fragments.shape, BF16),
            pltpu.VMEM((halves, total, LANES), F32),
            pltpu.VMEM((total, bins), BF16),
            pltpu.VMEM((total, bins), F32),
            pltpu.VMEM((max(total // LANES, 8), LANES), I32),
            pltpu.VMEM((blocks, LANES), F32),
            pltpu.VMEM((2 * nz, bins), F32),
            pltpu.VMEM((total, LANES), BF16),
            pltpu.VMEM((LANES, bins), BF16),
            pltpu.VMEM((columns, bins), F32),
            pltpu.VMEM(((nx - 2) * ny, bins), BF16),
            pltpu.VMEM((rim, bins), BF16),
            pltpu.VMEM((rim, bins), F32),
            dma((parts,)),
            dma((10,)),
            dma((1,)),
            dma((4,)),
            dma((4,)),
            dma((inner + 2,)),
            dma((inner + 2,)),
        ],
        compiler_params=pltpu.CompilerParams(
            collective_id=0, has_side_effects=True, vmem_limit_bytes=(60 << 20) - cells * bins * 4
        ),
        name="step",
    )(dense, *winds, fall_rate, listed, block_target, pair_inputs, pair_outputs, loss_kernel, fragments)

    slots = 8
    _, settled = pl.pallas_call(
        settle_kernel,
        out_shape=(
            pltpu.VMEM((halves, cells, LANES), F32),
            jax.ShapeDtypeStruct((nx, ny, packed, LANES), BF16),
        ),
        in_specs=[vmem] * 6,
        out_specs=(vmem, hbm),
        scratch_shapes=[
            pltpu.SMEM((width, blocks), I32),
            pltpu.VMEM((columns, bins), F32),
            pltpu.VMEM((nz, bins), F32),
            pltpu.VMEM((nz, bins), F32),
            pltpu.VMEM((slots, halves, ny * nz, LANES), F32),
            pltpu.VMEM((nx, ny, packed, LANES), BF16),
            dma((1,)),
            dma((nx // 2,)),
        ],
        input_output_aliases={0: 0},
        compiler_params=pltpu.CompilerParams(vmem_limit_bytes=32 << 20),
        name="settle",
    )(adv, moist, arrived, edge_in, spots, fall_v)
    return settled.reshape(nx, ny, halves, nz, LANES).transpose(0, 1, 3, 2, 4).reshape(nx, ny, nz, bins)


def solution(mesh):
    in_specs = (
        P("gx", "gy", "gz", None),
        P("gx", "gy", "gz"),
        P("gx", "gy", "gz"),
        P("gz", None),
        P("gx", "gy", "gz", None, None),
        P(None, None, "gz", None),
        P(),
        P(),
        P(),
        P(),
    )
    out_specs = P("gx", "gy", "gz", None)
    return jax.shard_map(body, mesh=mesh, in_specs=in_specs, out_specs=out_specs, check_vma=False)
```

```python
import functools

import jax
import jax.numpy as jnp
from jax import lax
from jax.experimental import pallas as pl
from jax.experimental.pallas import tpu as pltpu
from jax.sharding import PartitionSpec as P

MESH = pl.DeviceIdType.MESH
F32 = jnp.float32
BF16 = jnp.bfloat16
I32 = jnp.int32
LANES = 128
GROUP = 8


def spot_of(column, level, levels):
    return (column // GROUP * levels + level) * GROUP + column % GROUP


def step_kernel(
    spec, winds_e, winds_n, fall_h, cells_h, target_h, pair_in_h, pair_out_h, loss_h, frag_h,
    adv, moist, edge_moist, arrived, edge_in, spots, fall,
    local, we, wn, west, east, south, north, cells, listed_v, target, pair_in, pair_out, loss, frag,
    rows, q, pz, ids, places, live, shares, picks, table, settled, flux, edge_flux,
    load_sem, in_sem, spot_sem, send_sem, recv_sem, down_sem, got_sem,
):
    nx, ny, packed, _ = spec.shape
    nz, bins = fall.shape
    halves = bins // LANES
    width, blocks = cells.shape
    total = width * blocks
    pairs = pair_out.shape[0]
    parts = load_sem.shape[0]
    per = nx // parts
    gx, gy, me = lax.axis_index("gx"), lax.axis_index("gy"), lax.axis_index("gz")
    sx, sy, count = lax.axis_size("gx"), lax.axis_size("gy"), lax.axis_size("gz")
    plane = sx * sy
    top = count - 1
    to_west = {"gx": lax.rem(gx + sx - 1, sx)}
    to_east = {"gx": lax.rem(gx + 1, sx)}
    to_south = {"gy": lax.rem(gy + sy - 1, sy)}
    to_north = {"gy": lax.rem(gy + 1, sy)}
    above = {"gz": lax.rem(me + 1, count)}
    below = {"gz": lax.rem(me + top, count)}

    barrier = pltpu.get_barrier_semaphore()
    for peer in (to_west, to_east, to_south, to_north, above, below):
        pl.semaphore_signal(barrier, inc=1, device_id=peer, device_id_type=MESH)

    def fetch(i, src, dst):
        return pltpu.make_async_copy(src, dst, in_sem.at[i])

    wind_loads = [fetch(0, winds_e, we), fetch(1, winds_n, wn)]
    loads = [
        pltpu.make_async_copy(spec.at[pl.ds(p * per, per)], local.at[pl.ds(1 + p * per, per)], load_sem.at[p])
        for p in range(parts)
    ]
    small = [fetch(2, fall_h, fall), fetch(3, cells_h, listed_v), fetch(4, target_h, target)]
    weights = [
        fetch(6, pair_in_h, pair_in), fetch(7, pair_out_h, pair_out), fetch(8, loss_h, loss), fetch(9, frag_h, frag)
    ]
    for load in small + wind_loads + loads + weights:
        load.start()
    pl.semaphore_wait(barrier, 6)

    sends = [
        pltpu.make_async_remote_copy(
            src_ref=src,
            dst_ref=dst,
            send_sem=send_sem.at[i],
            recv_sem=recv_sem.at[i],
            device_id=peer,
            device_id_type=MESH,
        )
        for i, (src, dst, peer) in enumerate(
            (
                (spec.at[:, ny - 1], south, to_north),
                (spec.at[:, 0], north, to_south),
                (spec.at[nx - 1], west, to_east),
                (spec.at[0], east, to_west),
            )
        )
    ]
    for send in sends:
        send.start()

    zero_row = jnp.zeros((ny, packed, LANES), BF16)
    local[0] = zero_row
    local[nx + 1] = zero_row

    def stacked(tile):
        return jnp.concatenate([tile] * halves, axis=0).astype(BF16)

    def spread(tile, y):
        return jnp.broadcast_to(tile[:, y : y + 1], (packed, LANES))

    def total_of(terms):
        while len(terms) > 1:
            terms = [a + b for a, b in zip(terms[::2], terms[1::2])]
        return terms[0]

    def sink(x):
        for g in range(ny // GROUP):
            at = pl.ds(pl.multiple_of(x * ny + g * GROUP, GROUP), GROUP)
            base = pl.multiple_of((x * ny + g * GROUP) * nz, GROUP * nz)
            for h in range(halves):
                lanes = slice(h * LANES, (h + 1) * LANES)
                terms = [adv[h, pl.ds(base + z * GROUP, GROUP), :] * shares[z : z + 1, lanes] for z in range(nz)]
                settled[at, lanes] = total_of(terms)

    share_rows = total // nx

    def two_rows(i, carry):
        for turn in range(2):
            one_row(2 * i + turn)
        return carry

    def one_row(x):
        both = jnp.concatenate([we[x]] * (halves // 2) + [wn[x]] * (halves // 2), axis=0).astype(BF16)
        some = pl.ds(pl.multiple_of(x * share_rows, share_rows), share_rows)
        pz[some, :] = jnp.dot(picks[some, :], table[...], preferred_element_type=F32)
        sink(jnp.maximum(x - 1, 0))

        zero = jnp.zeros((packed, LANES), BF16)
        behind = zero
        centre = local[x + 1, 0]
        for y in range(ny):
            ahead = local[x + 1, y + 1] if y + 1 < ny else zero
            pair = spread(both, y)
            a = jnp.concatenate([pair[0:nz]] * halves, axis=0)
            b = jnp.concatenate([pair[nz : 2 * nz]] * halves, axis=0)
            up_x = jnp.where(a > 0, local[x, y], local[x + 2, y])
            up_y = jnp.where(b > 0, behind, ahead)
            change = jnp.abs(a) * (up_x - centre) + jnp.abs(b) * (up_y - centre)
            value = centre.astype(F32) + change.astype(F32)
            base = pl.multiple_of((x * ny + y - y % GROUP) * nz, GROUP * nz)
            for h in range(halves):
                adv[h, pl.ds(base + y % GROUP, nz, stride=GROUP), :] = value[h * nz : (h + 1) * nz]
            behind, centre = centre, ahead

    for load in small:
        load.wait()

    ratio = fall[...] / (1.0 + fall[...])
    share = jnp.ones((1, bins), F32)
    for z in range(nz):
        share = share * ratio[z : z + 1, :]
        shares[z : z + 1, :] = share
    shares[nz : 2 * nz, :] = ratio
    gain = share

    listed = listed_v[...]
    spots[...] = spot_of(listed // nz, listed % nz, nz)
    spot = pltpu.make_async_copy(spots, cells, spot_sem.at[0])
    spot.start()
    cloudy = target[gx, gy] < plane
    columns = jnp.where(cloudy, listed // nz, -1)
    cloudy_spots = jnp.where(cloudy, spots[...], -1)
    per_tile = LANES // blocks
    for t in range(total // LANES):
        for kept, found in ((ids, columns), (places, cloudy_spots)):
            lines = [found[t * per_tile + i : t * per_tile + i + 1, :] for i in range(per_tile)]
            kept[t : t + 1, :] = jnp.concatenate(lines, axis=1)
    flags = jnp.broadcast_to(jnp.where(cloudy, 1.0, 0.0), (8, blocks)).T
    live[...] = jnp.broadcast_to(flags[:, 0:1], (blocks, LANES))
    heights = (listed % nz).astype(F32).T
    high = shares[0:nz, :].astype(BF16)
    low = (shares[0:nz, :] - high.astype(F32)).astype(BF16)
    table[...] = jnp.concatenate([high, low, jnp.zeros((LANES - 2 * nz, bins), BF16)], axis=0)
    lane = lax.broadcasted_iota(I32, (blocks, LANES), 1)
    level_of = jnp.where(lane < 2 * nz, lane % nz, -1).astype(F32)
    for j in range(width):
        hit = jnp.broadcast_to(heights[:, j : j + 1], (blocks, LANES)) == level_of
        picks[j * blocks : (j + 1) * blocks, :] = jnp.where(hit, 1.0, 0.0).astype(BF16)

    for load in wind_loads:
        load.wait()
    done = 0
    for p in range(parts):
        loads[p].wait()
        upto = nx // 2 if p == parts - 1 else ((p + 1) * per - 1) // 2
        lax.fori_loop(done, upto, two_rows, 0)
        done = upto

    for load in weights:
        load.wait()

    size = min(512, total)
    tile = min(256, pairs)
    inner = down_sem.shape[0] - 2
    span = (nx - 2) // inner
    wide = span * ny

    def gather(i):
        for r in range(i * size, (i + 1) * size):
            cell = pl.ds(cells[r // blocks, r % blocks], 1)
            for h in range(halves):
                rows[h, r : r + 1, :] = adv[h, cell, :]

    def tendency_of(row):
        decline = jnp.dot(row, loss[...], preferred_element_type=F32)
        losses = row.astype(F32) * decline
        gained = jnp.dot(losses.astype(BF16), frag[...], preferred_element_type=F32)
        for n in range(0, pairs, tile):
            first = jnp.dot(row, pair_in[:, n : n + tile], preferred_element_type=F32)
            second = jnp.dot(row, pair_in[:, pairs + n : pairs + n + tile], preferred_element_type=F32)
            product = (first * second).astype(BF16)
            gained = gained + jnp.dot(product, pair_out[n : n + tile, :], preferred_element_type=F32)
        return (gained - losses).astype(BF16).astype(F32)

    def collide(i):
        at = slice(i * size, (i + 1) * size)
        full = jnp.concatenate([rows[h, at, :] for h in range(halves)], axis=1)
        alive = jnp.concatenate([jnp.concatenate([live[...]] * halves, axis=1)] * (size // blocks), axis=0)
        tendency = jnp.where(alive > 0.0, tendency_of(full.astype(BF16)), 0.0)
        q[at, :] = (tendency * pz[at, :]).astype(BF16)
        after = full + tendency
        for h in range(halves):
            moist[h, at, :] = after[:, h * LANES : (h + 1) * LANES]

    def listed_tile(first, apart):
        cell = lax.broadcasted_iota(I32, (GROUP, LANES), 0) * apart + first
        hit = jnp.broadcast_to(places[0:1, :], cell.shape) == cell
        for t in range(1, total // LANES):
            hit = hit | (jnp.broadcast_to(places[t : t + 1, :], cell.shape) == cell)
        found = jnp.max(jnp.where(hit, 1.0, 0.0), axis=1, keepdims=True)
        return jnp.broadcast_to(found, cell.shape)

    def rim_tiles(p):
        if p == inner:
            starts = [x * ny * nz + k * GROUP for x in (0, nx - 1) for k in range(ny * nz // GROUP)]
            return [(start, 1) for start in starts]
        return [(spot_of(x * ny + y, 0, nz), GROUP) for y in (0, ny - 1) for x in range(nx)]

    def collide_rim(p):
        tiles = rim_tiles(p)
        sides = []
        for h in range(halves):
            if p == inner:
                wanted = [adv[h, x * ny * nz : (x + 1) * ny * nz, :] for x in (0, nx - 1)]
            else:
                wanted = [adv[h, pl.ds(first, nz, stride=apart), :] for first, apart in tiles]
            sides.append(jnp.concatenate(wanted, axis=0))
        full = jnp.concatenate(sides, axis=1)
        alive = jnp.concatenate([listed_tile(first, apart) for first, apart in tiles], axis=0)
        alive = jnp.concatenate([alive] * halves, axis=1)
        after = full + jnp.where(alive > 0.0, tendency_of(full.astype(BF16)), 0.0)
        offset = 0 if p == inner else 2 * ny * nz
        for h in range(halves):
            edge_moist[h, offset : offset + full.shape[0], :] = after[:, h * LANES : (h + 1) * LANES]
        left = []
        if p == inner:
            for g in range(2 * ny // GROUP):
                level = [after[(g * nz + z) * GROUP : (g * nz + z + 1) * GROUP, :] * shares[z : z + 1, :] for z in range(nz)]
                left.append(total_of(level))
        else:
            for i in range(2 * nx):
                left.append(jnp.sum(after[i * nz : (i + 1) * nz, :] * shares[0:nz, :], axis=0, keepdims=True))
        edge_flux[edge[p], :] = jnp.concatenate(left, axis=0).astype(BF16)

    def collide_all():
        chunks = total // size
        gather(0)
        for i in range(chunks):
            if i + 1 < chunks:
                gather(i + 1)
            collide(i)

    def collected(column):
        hot = [
            jnp.where(jnp.broadcast_to(ids[t : t + 1, :], column.shape) == column, 1.0, 0.0).astype(BF16)
            for t in range(total // LANES)
        ]
        return jnp.dot(jnp.concatenate(hot, axis=1), q[...], preferred_element_type=F32)

    edge = {inner: slice(0, 2 * ny), inner + 1: slice(2 * ny, 2 * (ny + nx))}

    def down(p):
        src = edge_flux.at[edge[p]] if p in edge else flux.at[pl.ds(p * wide, wide)]
        dst = edge_in.at[edge[p]] if p in edge else arrived.at[pl.ds((1 + p * span) * ny, wide)]
        return pltpu.make_async_remote_copy(
            src_ref=src,
            dst_ref=dst,
            send_sem=down_sem.at[p],
            recv_sem=got_sem.at[p],
            device_id={"gz": jnp.maximum(me - 1, 0)},
            device_id_type=MESH,
        )

    def relay(p):
        down(p).wait_recv()

        @pl.when(me > 0)
        def _():
            if p in edge:
                at = edge[p]
                edge_flux[at, :] = (edge_flux[at, :].astype(F32) + edge_in[at, :].astype(F32) * gain).astype(BF16)
            else:
                at = pl.ds(p * wide, wide)
                got = arrived[pl.ds((1 + p * span) * ny, wide), :].astype(F32)
                flux[at, :] = (flux[at, :].astype(F32) + got * gain).astype(BF16)
            down(p).start()

    spot.wait()
    collide_all()

    for p in range(inner):
        half = wide // 2
        for part in range(2):
            start = p * wide + part * half
            column = lax.broadcasted_iota(I32, (half, LANES), 0) + (ny + start)
            held = settled[ny + start : ny + start + half, :]
            flux[start : start + half, :] = (collected(column) + held).astype(BF16)

        @pl.when(me == top)
        def _():
            down(p).start()

        @pl.when(me == top - 1)
        def _():
            relay(p)

    for send in sends[:2]:
        send.wait_recv()

    def add_halo(column, wind, halo):
        came = wind.astype(F32) * halo.astype(F32)
        at = pl.ds(spot_of(column, 0, nz), nz, stride=GROUP)
        for h in range(halves):
            adv[h, at, :] = adv[h, at, :] + came[h * nz : (h + 1) * nz]

    def edges(x, carry):
        winds = stacked(wn[x])
        add_halo(x * ny, jnp.maximum(spread(winds, 0), 0), south[x])
        add_halo(x * ny + ny - 1, jnp.maximum(-spread(winds, ny - 1), 0), north[x])
        return carry

    lax.fori_loop(0, nx, edges, 0, unroll=8)

    for send, x, halo, sign in ((sends[2], 0, west, 1.0), (sends[3], nx - 1, east, -1.0)):
        send.wait_recv()
        winds = jnp.maximum(sign * stacked(we[x]), 0)
        for y in range(ny):
            add_halo(x * ny + y, spread(winds, y), halo[y])

    for p in edge:
        collide_rim(p)

        @pl.when(me == top)
        def _():
            down(p).start()

    @pl.when(me == top)
    def _():
        arrived[...] = jnp.zeros(arrived.shape, BF16)
        edge_in[...] = jnp.zeros(edge_in.shape, BF16)

    @pl.when(me == top - 1)
    def _():
        for p in edge:
            relay(p)

    @pl.when(me < top - 1)
    def _():
        for p in range(inner + 2):
            relay(p)

    @pl.when(me > 0)
    def _():
        for p in range(inner + 2):
            down(p).wait_send()

    for send in sends:
        send.wait_send()


def settle_kernel(
    adv_in, moist, edge_moist, arrived, edge_in, spots, fall, adv, out, cells, flow, inverse, ratio, level_out, staged,
    cell_sem, out_sem
):
    nx, ny, packed, _ = out.shape
    nz, bins = fall.shape
    halves = bins // LANES
    width, blocks = cells.shape
    slots = level_out.shape[0]
    each = nx // out_sem.shape[0]

    fetch = pltpu.make_async_copy(spots, cells, cell_sem.at[0])
    fetch.start()
    inverse[...] = 1.0 / (1.0 + fall[...])
    ratio[...] = fall[...] * inverse[...]
    flow[...] = arrived[...].astype(F32)
    rim = edge_in[...].astype(F32)
    flow[0:ny, :] = rim[0:ny]
    flow[(nx - 1) * ny : nx * ny, :] = rim[ny : 2 * ny]
    for i in range(nx):
        flow[i * ny : i * ny + 1, :] = rim[2 * ny + i : 2 * ny + i + 1]
        flow[i * ny + ny - 1 : i * ny + ny, :] = rim[2 * ny + nx + i : 2 * ny + nx + i + 1]
    fetch.wait()

    for r in range(width * blocks):
        cell = pl.ds(cells[r // blocks, r % blocks], 1)
        for h in range(halves):
            adv[h, cell, :] = moist[h, r : r + 1, :]

    row = ny * nz
    for h in range(halves):
        for i, x in enumerate((0, nx - 1)):
            adv[h, x * row : (x + 1) * row, :] = edge_moist[h, i * row : (i + 1) * row, :]
        for i, y in enumerate((0, ny - 1)):
            for x in range(nx):
                came = (2 * ny + i * nx + x) * nz
                adv[h, pl.ds(spot_of(x * ny + y, 0, nz), nz, stride=GROUP), :] = edge_moist[h, came : came + nz, :]

    def push(i):
        at = pl.ds(i * each, each)
        return pltpu.make_async_copy(staged.at[at], out.at[at], out_sem.at[i])

    def some_rows(i, carry):
        for slot in range(slots):
            x = i * slots + slot
            for g in range(ny // GROUP):
                column = pl.multiple_of(x * ny + g * GROUP, GROUP)
                for h in range(halves):
                    lanes = slice(h * LANES, (h + 1) * LANES)
                    inflow = flow[pl.ds(column, GROUP), lanes]
                    for z in reversed(range(nz)):
                        held = adv[h, pl.ds(pl.multiple_of(column * nz + z * GROUP, GROUP), GROUP), :] + inflow
                        to = pl.ds(g * GROUP * nz + z, GROUP, stride=nz)
                        level_out[slot, h, to, :] = held * inverse[z : z + 1, lanes]
                        inflow = held * ratio[z : z + 1, lanes]
            for y in range(ny):
                pieces = [level_out[slot, h, y * nz : (y + 1) * nz, :] for h in range(halves)]
                staged[x, y] = jnp.concatenate(pieces, axis=0).astype(BF16)
            if (slot + 1) % each == 0:
                push((x + 1) // each - 1).start()
        return carry

    lax.fori_loop(0, nx // slots, some_rows, 0)
    for i in range(nx // each):
        push(i).wait()


def body(
    spectrum,
    wind_east,
    wind_north,
    fall_rate,
    cloud_cells,
    block_target,
    pair_inputs,
    pair_outputs,
    loss_kernel,
    fragments,
):
    nx, ny, nz, bins = spectrum.shape
    halves = bins // LANES
    cells = nx * ny * nz
    columns = nx * ny
    blocks, width = cloud_cells.shape[3], cloud_cells.shape[4]
    total = blocks * width
    pairs = pair_outputs.shape[0]
    packed = nz * halves
    winds = (wind_east.transpose(0, 2, 1), wind_north.transpose(0, 2, 1))
    listed = cloud_cells.reshape(blocks, width).T
    dma = pltpu.SemaphoreType.DMA
    hbm = pl.BlockSpec(memory_space=pltpu.HBM)
    vmem = pl.BlockSpec(memory_space=pltpu.VMEM)
    dense = spectrum.reshape(nx, ny, nz, halves, LANES).transpose(0, 1, 3, 2, 4).reshape(nx, ny, packed, LANES)
    span = max(s for s in range(1, 7) if (nx - 2) % s == 0)
    inner = (nx - 2) // span
    rim = 2 * (nx + ny)
    parts = 4

    adv, moist, edge_moist, arrived, edge_in, spots, fall_v = pl.pallas_call(
        step_kernel,
        out_shape=(
            pltpu.VMEM((halves, cells, LANES), F32),
            pltpu.VMEM((halves, total, LANES), F32),
            pltpu.VMEM((halves, rim * nz, LANES), F32),
            pltpu.VMEM((columns, bins), BF16),
            pltpu.VMEM((rim, bins), BF16),
            pltpu.VMEM((width, blocks), I32),
            pltpu.VMEM(fall_rate.shape, F32),
        ),
        in_specs=[hbm] * 10,
        out_specs=(vmem,) * 7,
        scratch_shapes=[
            pltpu.VMEM((nx + 2, ny, packed, LANES), BF16),
            pltpu.VMEM(winds[0].shape, F32),
            pltpu.VMEM(winds[1].shape, F32),
            pltpu.VMEM((ny, packed, LANES), BF16),
            pltpu.VMEM((ny, packed, LANES), BF16),
            pltpu.VMEM((nx, packed, LANES), BF16),
            pltpu.VMEM((nx, packed, LANES), BF16),
            pltpu.SMEM((width, blocks), I32),
            pltpu.VMEM((width, blocks), I32),
            pltpu.VMEM(block_target.shape, I32),
            pltpu.VMEM(pair_inputs.shape, BF16),
            pltpu.VMEM(pair_outputs.shape, BF16),
            pltpu.VMEM(loss_kernel.shape, BF16),
            pltpu.VMEM(fragments.shape, BF16),
            pltpu.VMEM((halves, total, LANES), F32),
            pltpu.VMEM((total, bins), BF16),
            pltpu.VMEM((total, bins), F32),
            pltpu.VMEM((max(total // LANES, 8), LANES), I32),
            pltpu.VMEM((max(total // LANES, 8), LANES), I32),
            pltpu.VMEM((blocks, LANES), F32),
            pltpu.VMEM((2 * nz, bins), F32),
            pltpu.VMEM((total, LANES), BF16),
            pltpu.VMEM((LANES, bins), BF16),
            pltpu.VMEM((columns, bins), F32),
            pltpu.VMEM(((nx - 2) * ny, bins), BF16),
            pltpu.VMEM((rim, bins), BF16),
            dma((parts,)),
            dma((10,)),
            dma((1,)),
            dma((4,)),
            dma((4,)),
            dma((inner + 2,)),
            dma((inner + 2,)),
        ],
        compiler_params=pltpu.CompilerParams(
            collective_id=0, has_side_effects=True, vmem_limit_bytes=(60 << 20) - cells * bins * 4
        ),
        name="step",
    )(dense, *winds, fall_rate, listed, block_target, pair_inputs, pair_outputs, loss_kernel, fragments)

    slots = 8
    _, settled = pl.pallas_call(
        settle_kernel,
        out_shape=(
            pltpu.VMEM((halves, cells, LANES), F32),
            jax.ShapeDtypeStruct((nx, ny, packed, LANES), BF16),
        ),
        in_specs=[vmem] * 7,
        out_specs=(vmem, hbm),
        scratch_shapes=[
            pltpu.SMEM((width, blocks), I32),
            pltpu.VMEM((columns, bins), F32),
            pltpu.VMEM((nz, bins), F32),
            pltpu.VMEM((nz, bins), F32),
            pltpu.VMEM((slots, halves, ny * nz, LANES), F32),
            pltpu.VMEM((nx, ny, packed, LANES), BF16),
            dma((1,)),
            dma((nx // 2,)),
        ],
        input_output_aliases={0: 0},
        compiler_params=pltpu.CompilerParams(vmem_limit_bytes=32 << 20),
        name="settle",
    )(adv, moist, edge_moist, arrived, edge_in, spots, fall_v)
    return settled.reshape(nx, ny, halves, nz, LANES).transpose(0, 1, 3, 2, 4).reshape(nx, ny, nz, bins)


def solution(mesh):
    in_specs = (
        P("gx", "gy", "gz", None),
        P("gx", "gy", "gz"),
        P("gx", "gy", "gz"),
        P("gz", None),
        P("gx", "gy", "gz", None, None),
        P(None, None, "gz", None),
        P(),
        P(),
        P(),
        P(),
    )
    out_specs = P("gx", "gy", "gz", None)
    return jax.shard_map(body, mesh=mesh, in_specs=in_specs, out_specs=out_specs, check_vma=False)
```

```python
import functools

import jax
import jax.numpy as jnp
from jax import lax
from jax.experimental import pallas as pl
from jax.experimental.pallas import tpu as pltpu
from jax.sharding import PartitionSpec as P

MESH = pl.DeviceIdType.MESH
F32 = jnp.float32
BF16 = jnp.bfloat16
I32 = jnp.int32
LANES = 128
GROUP = 8


def spot_of(column, level, levels):
    return (column // GROUP * levels + level) * GROUP + column % GROUP


def step_kernel(
    spec, winds_e, winds_n, fall_h, cells_h, target_h, pair_in_h, pair_out_h, loss_h, frag_h,
    adv, moist, edge_moist, arrived, edge_in, spots, fall,
    local, we, wn, west, east, south, north, cells, listed_v, target, pair_in, pair_out, loss, frag,
    rows, q, pz, ids, places, live, shares, picks, table, settled, flux, edge_flux,
    load_sem, in_sem, spot_sem, send_sem, recv_sem, down_sem, got_sem,
):
    nx, ny, packed, _ = spec.shape
    nz, bins = fall.shape
    halves = bins // LANES
    width, blocks = cells.shape
    total = width * blocks
    pairs = pair_out.shape[0]
    parts = load_sem.shape[0]
    per = nx // parts
    gx, gy, me = lax.axis_index("gx"), lax.axis_index("gy"), lax.axis_index("gz")
    sx, sy, count = lax.axis_size("gx"), lax.axis_size("gy"), lax.axis_size("gz")
    plane = sx * sy
    top = count - 1
    to_west = {"gx": lax.rem(gx + sx - 1, sx)}
    to_east = {"gx": lax.rem(gx + 1, sx)}
    to_south = {"gy": lax.rem(gy + sy - 1, sy)}
    to_north = {"gy": lax.rem(gy + 1, sy)}
    above = {"gz": lax.rem(me + 1, count)}
    below = {"gz": lax.rem(me + top, count)}

    barrier = pltpu.get_barrier_semaphore()
    for peer in (to_west, to_east, to_south, to_north, above, below):
        pl.semaphore_signal(barrier, inc=1, device_id=peer, device_id_type=MESH)

    def fetch(i, src, dst):
        return pltpu.make_async_copy(src, dst, in_sem.at[i])

    wind_loads = [fetch(0, winds_e, we), fetch(1, winds_n, wn)]
    loads = [
        pltpu.make_async_copy(spec.at[pl.ds(p * per, per)], local.at[pl.ds(1 + p * per, per)], load_sem.at[p])
        for p in range(parts)
    ]
    small = [fetch(2, fall_h, fall), fetch(3, cells_h, listed_v), fetch(4, target_h, target)]
    weights = [
        fetch(6, pair_in_h, pair_in), fetch(7, pair_out_h, pair_out), fetch(8, loss_h, loss), fetch(9, frag_h, frag)
    ]
    for load in small + wind_loads + loads + weights:
        load.start()
    pl.semaphore_wait(barrier, 6)

    sends = [
        pltpu.make_async_remote_copy(
            src_ref=src,
            dst_ref=dst,
            send_sem=send_sem.at[i],
            recv_sem=recv_sem.at[i],
            device_id=peer,
            device_id_type=MESH,
        )
        for i, (src, dst, peer) in enumerate(
            (
                (spec.at[:, ny - 1], south, to_north),
                (spec.at[:, 0], north, to_south),
                (spec.at[nx - 1], west, to_east),
                (spec.at[0], east, to_west),
            )
        )
    ]
    for send in sends:
        send.start()

    zero_row = jnp.zeros((ny, packed, LANES), BF16)
    local[0] = zero_row
    local[nx + 1] = zero_row

    def stacked(tile):
        return jnp.concatenate([tile] * halves, axis=0).astype(BF16)

    def spread(tile, y):
        return jnp.broadcast_to(tile[:, y : y + 1], (packed, LANES))

    def total_of(terms):
        while len(terms) > 1:
            terms = [a + b for a, b in zip(terms[::2], terms[1::2])]
        return terms[0]

    def sink(x):
        for g in range(ny // GROUP):
            at = pl.ds(pl.multiple_of(x * ny + g * GROUP, GROUP), GROUP)
            base = pl.multiple_of((x * ny + g * GROUP) * nz, GROUP * nz)
            for h in range(halves):
                lanes = slice(h * LANES, (h + 1) * LANES)
                terms = [adv[h, pl.ds(base + z * GROUP, GROUP), :] * shares[z : z + 1, lanes] for z in range(nz)]
                settled[at, lanes] = total_of(terms)

    share_rows = total // nx

    def two_rows(i, carry):
        for turn in range(2):
            one_row(2 * i + turn)
        return carry

    def one_row(x):
        both = jnp.concatenate([we[x]] * (halves // 2) + [wn[x]] * (halves // 2), axis=0).astype(BF16)
        some = pl.ds(pl.multiple_of(x * share_rows, share_rows), share_rows)
        pz[some, :] = jnp.dot(picks[some, :], table[...], preferred_element_type=F32)
        sink(jnp.maximum(x - 1, 0))

        zero = jnp.zeros((packed, LANES), BF16)
        behind = zero
        centre = local[x + 1, 0]
        for y in range(ny):
            ahead = local[x + 1, y + 1] if y + 1 < ny else zero
            pair = spread(both, y)
            a = jnp.concatenate([pair[0:nz]] * halves, axis=0)
            b = jnp.concatenate([pair[nz : 2 * nz]] * halves, axis=0)
            up_x = jnp.where(a > 0, local[x, y], local[x + 2, y])
            up_y = jnp.where(b > 0, behind, ahead)
            change = jnp.abs(a) * (up_x - centre) + jnp.abs(b) * (up_y - centre)
            value = centre.astype(F32) + change.astype(F32)
            base = pl.multiple_of((x * ny + y - y % GROUP) * nz, GROUP * nz)
            for h in range(halves):
                adv[h, pl.ds(base + y % GROUP, nz, stride=GROUP), :] = value[h * nz : (h + 1) * nz]
            behind, centre = centre, ahead

    for load in small:
        load.wait()

    ratio = fall[...] / (1.0 + fall[...])
    share = jnp.ones((1, bins), F32)
    for z in range(nz):
        share = share * ratio[z : z + 1, :]
        shares[z : z + 1, :] = share
    shares[nz : 2 * nz, :] = ratio
    gain = share

    listed = listed_v[...]
    spots[...] = spot_of(listed // nz, listed % nz, nz)
    spot = pltpu.make_async_copy(spots, cells, spot_sem.at[0])
    spot.start()
    cloudy = target[gx, gy] < plane
    columns = jnp.where(cloudy, listed // nz, -1)
    cloudy_spots = jnp.where(cloudy, spots[...], -1)
    per_tile = LANES // blocks
    for t in range(total // LANES):
        for kept, found in ((ids, columns), (places, cloudy_spots)):
            lines = [found[t * per_tile + i : t * per_tile + i + 1, :] for i in range(per_tile)]
            kept[t : t + 1, :] = jnp.concatenate(lines, axis=1)
    flags = jnp.broadcast_to(jnp.where(cloudy, 1.0, 0.0), (8, blocks)).T
    live[...] = jnp.broadcast_to(flags[:, 0:1], (blocks, LANES))
    heights = (listed % nz).astype(F32).T
    high = shares[0:nz, :].astype(BF16)
    low = (shares[0:nz, :] - high.astype(F32)).astype(BF16)
    table[...] = jnp.concatenate([high, low, jnp.zeros((LANES - 2 * nz, bins), BF16)], axis=0)
    lane = lax.broadcasted_iota(I32, (blocks, LANES), 1)
    level_of = jnp.where(lane < 2 * nz, lane % nz, -1).astype(F32)
    for j in range(width):
        hit = jnp.broadcast_to(heights[:, j : j + 1], (blocks, LANES)) == level_of
        picks[j * blocks : (j + 1) * blocks, :] = jnp.where(hit, 1.0, 0.0).astype(BF16)

    for load in wind_loads:
        load.wait()
    done = 0
    for p in range(parts):
        loads[p].wait()
        upto = nx // 2 if p == parts - 1 else ((p + 1) * per - 1) // 2
        lax.fori_loop(done, upto, two_rows, 0)
        done = upto

    for load in weights:
        load.wait()

    size = min(512, total)
    tile = min(256, pairs)
    inner = down_sem.shape[0] - 2
    span = (nx - 2) // inner
    wide = span * ny

    def gather(i):
        for r in range(i * size, (i + 1) * size):
            cell = pl.ds(cells[r // blocks, r % blocks], 1)
            for h in range(halves):
                rows[h, r : r + 1, :] = adv[h, cell, :]

    def tendency_of(row):
        decline = jnp.dot(row, loss[...], preferred_element_type=F32)
        losses = row.astype(F32) * decline
        gained = jnp.dot(losses.astype(BF16), frag[...], preferred_element_type=F32)
        for n in range(0, pairs, tile):
            first = jnp.dot(row, pair_in[:, n : n + tile], preferred_element_type=F32)
            second = jnp.dot(row, pair_in[:, pairs + n : pairs + n + tile], preferred_element_type=F32)
            product = (first * second).astype(BF16)
            gained = gained + jnp.dot(product, pair_out[n : n + tile, :], preferred_element_type=F32)
        return (gained - losses).astype(BF16).astype(F32)

    def collide(i):
        at = slice(i * size, (i + 1) * size)
        full = jnp.concatenate([rows[h, at, :] for h in range(halves)], axis=1)
        alive = jnp.concatenate([jnp.concatenate([live[...]] * halves, axis=1)] * (size // blocks), axis=0)
        tendency = jnp.where(alive > 0.0, tendency_of(full.astype(BF16)), 0.0)
        q[at, :] = (tendency * pz[at, :]).astype(BF16)
        after = full + tendency
        for h in range(halves):
            moist[h, at, :] = after[:, h * LANES : (h + 1) * LANES]

    def listed_tile(first, apart):
        cell = lax.broadcasted_iota(I32, (GROUP, LANES), 0) * apart + first
        hit = jnp.broadcast_to(places[0:1, :], cell.shape) == cell
        for t in range(1, total // LANES):
            hit = hit | (jnp.broadcast_to(places[t : t + 1, :], cell.shape) == cell)
        found = jnp.max(jnp.where(hit, 1.0, 0.0), axis=1, keepdims=True)
        return jnp.broadcast_to(found, cell.shape)

    def rim_tiles(p):
        if p == inner:
            starts = [x * ny * nz + k * GROUP for x in (0, nx - 1) for k in range(ny * nz // GROUP)]
            return [(start, 1) for start in starts]
        return [(spot_of(x * ny + y, 0, nz), GROUP) for y in (0, ny - 1) for x in range(nx)]

    def collide_rim(p):
        tiles = rim_tiles(p)
        sides = []
        for h in range(halves):
            if p == inner:
                wanted = [adv[h, x * ny * nz : (x + 1) * ny * nz, :] for x in (0, nx - 1)]
            else:
                wanted = [adv[h, pl.ds(first, nz, stride=apart), :] for first, apart in tiles]
            sides.append(jnp.concatenate(wanted, axis=0))
        full = jnp.concatenate(sides, axis=1)
        alive = jnp.concatenate([listed_tile(first, apart) for first, apart in tiles], axis=0)
        alive = jnp.concatenate([alive] * halves, axis=1)
        after = full + jnp.where(alive > 0.0, tendency_of(full.astype(BF16)), 0.0)
        offset = 0 if p == inner else 2 * ny * nz
        for h in range(halves):
            edge_moist[h, offset : offset + full.shape[0], :] = after[:, h * LANES : (h + 1) * LANES]
        left = []
        if p == inner:
            for g in range(2 * ny // GROUP):
                level = [after[(g * nz + z) * GROUP : (g * nz + z + 1) * GROUP, :] * shares[z : z + 1, :] for z in range(nz)]
                left.append(total_of(level))
        else:
            for i in range(2 * nx):
                left.append(jnp.sum(after[i * nz : (i + 1) * nz, :] * shares[0:nz, :], axis=0, keepdims=True))
        edge_flux[edge[p], :] = jnp.concatenate(left, axis=0).astype(BF16)

    def collide_all():
        chunks = total // size
        gather(0)
        for i in range(chunks):
            if i + 1 < chunks:
                gather(i + 1)
            collide(i)

    def collected(column):
        hot = [
            jnp.where(jnp.broadcast_to(ids[t : t + 1, :], column.shape) == column, 1.0, 0.0).astype(BF16)
            for t in range(total // LANES)
        ]
        return jnp.dot(jnp.concatenate(hot, axis=1), q[...], preferred_element_type=F32)

    edge = {inner: slice(0, 2 * ny), inner + 1: slice(2 * ny, 2 * (ny + nx))}

    def down(p):
        src = edge_flux.at[edge[p]] if p in edge else flux.at[pl.ds(p * wide, wide)]
        dst = edge_in.at[edge[p]] if p in edge else arrived.at[pl.ds((1 + p * span) * ny, wide)]
        return pltpu.make_async_remote_copy(
            src_ref=src,
            dst_ref=dst,
            send_sem=down_sem.at[p],
            recv_sem=got_sem.at[p],
            device_id={"gz": jnp.maximum(me - 1, 0)},
            device_id_type=MESH,
        )

    def relay(p):
        down(p).wait_recv()

        @pl.when(me > 0)
        def _():
            if p in edge:
                at = edge[p]
                edge_flux[at, :] = (edge_flux[at, :].astype(F32) + edge_in[at, :].astype(F32) * gain).astype(BF16)
            else:
                at = pl.ds(p * wide, wide)
                got = arrived[pl.ds((1 + p * span) * ny, wide), :].astype(F32)
                flux[at, :] = (flux[at, :].astype(F32) + got * gain).astype(BF16)
            down(p).start()

    spot.wait()
    collide_all()

    for p in range(inner):
        half = wide // 2
        for part in range(2):
            start = p * wide + part * half
            column = lax.broadcasted_iota(I32, (half, LANES), 0) + (ny + start)
            held = settled[ny + start : ny + start + half, :]
            flux[start : start + half, :] = (collected(column) + held).astype(BF16)

        @pl.when(me == top)
        def _():
            down(p).start()

        @pl.when(me == top - 1)
        def _():
            relay(p)

    for send in sends[:2]:
        send.wait_recv()

    def add_halo(column, wind, halo):
        came = wind.astype(F32) * halo.astype(F32)
        at = pl.ds(spot_of(column, 0, nz), nz, stride=GROUP)
        for h in range(halves):
            adv[h, at, :] = adv[h, at, :] + came[h * nz : (h + 1) * nz]

    def edges(x, carry):
        winds = stacked(wn[x])
        add_halo(x * ny, jnp.maximum(spread(winds, 0), 0), south[x])
        add_halo(x * ny + ny - 1, jnp.maximum(-spread(winds, ny - 1), 0), north[x])
        return carry

    lax.fori_loop(0, nx, edges, 0, unroll=8)

    for send, x, halo, sign in ((sends[2], 0, west, 1.0), (sends[3], nx - 1, east, -1.0)):
        send.wait_recv()
        winds = jnp.maximum(sign * stacked(we[x]), 0)
        for y in range(ny):
            add_halo(x * ny + y, spread(winds, y), halo[y])

    for p in edge:
        collide_rim(p)

    @pl.when(me == top)
    def _():
        for p in edge:
            down(p).start()
        arrived[...] = jnp.zeros(arrived.shape, BF16)
        edge_in[...] = jnp.zeros(edge_in.shape, BF16)

    @pl.when(me == top - 1)
    def _():
        for p in edge:
            relay(p)

    @pl.when(me < top - 1)
    def _():
        for p in range(inner + 2):
            relay(p)

    @pl.when(me > 0)
    def _():
        for p in range(inner + 2):
            down(p).wait_send()

    for send in sends:
        send.wait_send()


def settle_kernel(
    adv_in, moist, edge_moist, arrived, edge_in, spots, fall, adv, out, cells, flow, inverse, ratio, level_out, staged,
    cell_sem, out_sem
):
    nx, ny, packed, _ = out.shape
    nz, bins = fall.shape
    halves = bins // LANES
    width, blocks = cells.shape
    slots = level_out.shape[0]
    each = nx // out_sem.shape[0]

    fetch = pltpu.make_async_copy(spots, cells, cell_sem.at[0])
    fetch.start()
    inverse[...] = 1.0 / (1.0 + fall[...])
    ratio[...] = fall[...] * inverse[...]
    flow[...] = arrived[...].astype(F32)
    rim = edge_in[...].astype(F32)
    flow[0:ny, :] = rim[0:ny]
    flow[(nx - 1) * ny : nx * ny, :] = rim[ny : 2 * ny]
    for i in range(nx):
        flow[i * ny : i * ny + 1, :] = rim[2 * ny + i : 2 * ny + i + 1]
        flow[i * ny + ny - 1 : i * ny + ny, :] = rim[2 * ny + nx + i : 2 * ny + nx + i + 1]
    fetch.wait()

    for r in range(width * blocks):
        cell = pl.ds(cells[r // blocks, r % blocks], 1)
        for h in range(halves):
            adv[h, cell, :] = moist[h, r : r + 1, :]

    row = ny * nz
    for h in range(halves):
        for i, x in enumerate((0, nx - 1)):
            adv[h, x * row : (x + 1) * row, :] = edge_moist[h, i * row : (i + 1) * row, :]
        for i, y in enumerate((0, ny - 1)):
            for x in range(nx):
                came = (2 * ny + i * nx + x) * nz
                adv[h, pl.ds(spot_of(x * ny + y, 0, nz), nz, stride=GROUP), :] = edge_moist[h, came : came + nz, :]

    def push(i):
        at = pl.ds(i * each, each)
        return pltpu.make_async_copy(staged.at[at], out.at[at], out_sem.at[i])

    def some_rows(i, carry):
        for slot in range(slots):
            x = i * slots + slot
            for g in range(ny // GROUP):
                column = pl.multiple_of(x * ny + g * GROUP, GROUP)
                for h in range(halves):
                    lanes = slice(h * LANES, (h + 1) * LANES)
                    inflow = flow[pl.ds(column, GROUP), lanes]
                    for z in reversed(range(nz)):
                        held = adv[h, pl.ds(pl.multiple_of(column * nz + z * GROUP, GROUP), GROUP), :] + inflow
                        to = pl.ds(g * GROUP * nz + z, GROUP, stride=nz)
                        level_out[slot, h, to, :] = held * inverse[z : z + 1, lanes]
                        inflow = held * ratio[z : z + 1, lanes]
            for y in range(ny):
                pieces = [level_out[slot, h, y * nz : (y + 1) * nz, :] for h in range(halves)]
                staged[x, y] = jnp.concatenate(pieces, axis=0).astype(BF16)
            if (slot + 1) % each == 0:
                push((x + 1) // each - 1).start()
        return carry

    lax.fori_loop(0, nx // slots, some_rows, 0)
    for i in range(nx // each):
        push(i).wait()


def body(
    spectrum,
    wind_east,
    wind_north,
    fall_rate,
    cloud_cells,
    block_target,
    pair_inputs,
    pair_outputs,
    loss_kernel,
    fragments,
):
    nx, ny, nz, bins = spectrum.shape
    halves = bins // LANES
    cells = nx * ny * nz
    columns = nx * ny
    blocks, width = cloud_cells.shape[3], cloud_cells.shape[4]
    total = blocks * width
    pairs = pair_outputs.shape[0]
    packed = nz * halves
    winds = (wind_east.transpose(0, 2, 1), wind_north.transpose(0, 2, 1))
    listed = cloud_cells.reshape(blocks, width).T
    dma = pltpu.SemaphoreType.DMA
    hbm = pl.BlockSpec(memory_space=pltpu.HBM)
    vmem = pl.BlockSpec(memory_space=pltpu.VMEM)
    dense = spectrum.reshape(nx, ny, nz, halves, LANES).transpose(0, 1, 3, 2, 4).reshape(nx, ny, packed, LANES)
    span = max(s for s in range(1, 11) if (nx - 2) % s == 0)
    inner = (nx - 2) // span
    rim = 2 * (nx + ny)
    parts = 4

    adv, moist, edge_moist, arrived, edge_in, spots, fall_v = pl.pallas_call(
        step_kernel,
        out_shape=(
            pltpu.VMEM((halves, cells, LANES), F32),
            pltpu.VMEM((halves, total, LANES), F32),
            pltpu.VMEM((halves, rim * nz, LANES), F32),
            pltpu.VMEM((columns, bins), BF16),
            pltpu.VMEM((rim, bins), BF16),
            pltpu.VMEM((width, blocks), I32),
            pltpu.VMEM(fall_rate.shape, F32),
        ),
        in_specs=[hbm] * 10,
        out_specs=(vmem,) * 7,
        scratch_shapes=[
            pltpu.VMEM((nx + 2, ny, packed, LANES), BF16),
            pltpu.VMEM(winds[0].shape, F32),
            pltpu.VMEM(winds[1].shape, F32),
            pltpu.VMEM((ny, packed, LANES), BF16),
            pltpu.VMEM((ny, packed, LANES), BF16),
            pltpu.VMEM((nx, packed, LANES), BF16),
            pltpu.VMEM((nx, packed, LANES), BF16),
            pltpu.SMEM((width, blocks), I32),
            pltpu.VMEM((width, blocks), I32),
            pltpu.VMEM(block_target.shape, I32),
            pltpu.VMEM(pair_inputs.shape, BF16),
            pltpu.VMEM(pair_outputs.shape, BF16),
            pltpu.VMEM(loss_kernel.shape, BF16),
            pltpu.VMEM(fragments.shape, BF16),
            pltpu.VMEM((halves, total, LANES), F32),
            pltpu.VMEM((total, bins), BF16),
            pltpu.VMEM((total, bins), F32),
            pltpu.VMEM((max(total // LANES, 8), LANES), I32),
            pltpu.VMEM((max(total // LANES, 8), LANES), I32),
            pltpu.VMEM((blocks, LANES), F32),
            pltpu.VMEM((2 * nz, bins), F32),
            pltpu.VMEM((total, LANES), BF16),
            pltpu.VMEM((LANES, bins), BF16),
            pltpu.VMEM((columns, bins), F32),
            pltpu.VMEM(((nx - 2) * ny, bins), BF16),
            pltpu.VMEM((rim, bins), BF16),
            dma((parts,)),
            dma((10,)),
            dma((1,)),
            dma((4,)),
            dma((4,)),
            dma((inner + 2,)),
            dma((inner + 2,)),
        ],
        compiler_params=pltpu.CompilerParams(
            collective_id=0, has_side_effects=True, vmem_limit_bytes=(60 << 20) - cells * bins * 4
        ),
        name="step",
    )(dense, *winds, fall_rate, listed, block_target, pair_inputs, pair_outputs, loss_kernel, fragments)

    slots = 8
    _, settled = pl.pallas_call(
        settle_kernel,
        out_shape=(
            pltpu.VMEM((halves, cells, LANES), F32),
            jax.ShapeDtypeStruct((nx, ny, packed, LANES), BF16),
        ),
        in_specs=[vmem] * 7,
        out_specs=(vmem, hbm),
        scratch_shapes=[
            pltpu.SMEM((width, blocks), I32),
            pltpu.VMEM((columns, bins), F32),
            pltpu.VMEM((nz, bins), F32),
            pltpu.VMEM((nz, bins), F32),
            pltpu.VMEM((slots, halves, ny * nz, LANES), F32),
            pltpu.VMEM((nx, ny, packed, LANES), BF16),
            dma((1,)),
            dma((nx // 2,)),
        ],
        input_output_aliases={0: 0},
        compiler_params=pltpu.CompilerParams(vmem_limit_bytes=32 << 20),
        name="settle",
    )(adv, moist, edge_moist, arrived, edge_in, spots, fall_v)
    return settled.reshape(nx, ny, halves, nz, LANES).transpose(0, 1, 3, 2, 4).reshape(nx, ny, nz, bins)


def solution(mesh):
    in_specs = (
        P("gx", "gy", "gz", None),
        P("gx", "gy", "gz"),
        P("gx", "gy", "gz"),
        P("gz", None),
        P("gx", "gy", "gz", None, None),
        P(None, None, "gz", None),
        P(),
        P(),
        P(),
        P(),
    )
    out_specs = P("gx", "gy", "gz", None)
    return jax.shard_map(body, mesh=mesh, in_specs=in_specs, out_specs=out_specs, check_vma=False)
```

```python
import functools

import jax
import jax.numpy as jnp
from jax import lax
from jax.experimental import pallas as pl
from jax.experimental.pallas import tpu as pltpu
from jax.sharding import PartitionSpec as P

MESH = pl.DeviceIdType.MESH
F32 = jnp.float32
BF16 = jnp.bfloat16
I32 = jnp.int32
LANES = 128
GROUP = 8


def spot_of(column, level, levels):
    return (column // GROUP * levels + level) * GROUP + column % GROUP


def step_kernel(
    spec, winds_e, winds_n, fall_h, cells_h, target_h, pair_in_h, pair_out_h, loss_h, frag_h,
    adv, moist, edge_moist, arrived, edge_in, spots, fall,
    local, we, wn, west, east, south, north, cells, listed_v, target, pair_in, pair_out, loss, frag,
    rows, q, pz, ids, places, live, shares, picks, table, settled, flux, edge_flux,
    load_sem, in_sem, spot_sem, send_sem, recv_sem, down_sem, got_sem,
):
    nx, ny, packed, _ = spec.shape
    nz, bins = fall.shape
    halves = bins // LANES
    width, blocks = cells.shape
    total = width * blocks
    pairs = pair_out.shape[0]
    parts = load_sem.shape[0]
    per = nx // parts
    gx, gy, me = lax.axis_index("gx"), lax.axis_index("gy"), lax.axis_index("gz")
    sx, sy, count = lax.axis_size("gx"), lax.axis_size("gy"), lax.axis_size("gz")
    plane = sx * sy
    top = count - 1
    to_west = {"gx": lax.rem(gx + sx - 1, sx)}
    to_east = {"gx": lax.rem(gx + 1, sx)}
    to_south = {"gy": lax.rem(gy + sy - 1, sy)}
    to_north = {"gy": lax.rem(gy + 1, sy)}
    above = {"gz": lax.rem(me + 1, count)}
    below = {"gz": lax.rem(me + top, count)}

    barrier = pltpu.get_barrier_semaphore()
    for peer in (to_west, to_east, to_south, to_north, above, below):
        pl.semaphore_signal(barrier, inc=1, device_id=peer, device_id_type=MESH)

    def fetch(i, src, dst):
        return pltpu.make_async_copy(src, dst, in_sem.at[i])

    wind_loads = [fetch(0, winds_e, we), fetch(1, winds_n, wn)]
    loads = [
        pltpu.make_async_copy(spec.at[pl.ds(p * per, per)], local.at[pl.ds(1 + p * per, per)], load_sem.at[p])
        for p in range(parts)
    ]
    small = [fetch(2, fall_h, fall), fetch(3, cells_h, listed_v), fetch(4, target_h, target)]
    weights = [
        fetch(6, pair_in_h, pair_in), fetch(7, pair_out_h, pair_out), fetch(8, loss_h, loss), fetch(9, frag_h, frag)
    ]
    for load in small + wind_loads + loads + weights:
        load.start()
    pl.semaphore_wait(barrier, 6)

    sends = [
        pltpu.make_async_remote_copy(
            src_ref=src,
            dst_ref=dst,
            send_sem=send_sem.at[i],
            recv_sem=recv_sem.at[i],
            device_id=peer,
            device_id_type=MESH,
        )
        for i, (src, dst, peer) in enumerate(
            (
                (spec.at[:, ny - 1], south, to_north),
                (spec.at[:, 0], north, to_south),
                (spec.at[nx - 1], west, to_east),
                (spec.at[0], east, to_west),
            )
        )
    ]
    for send in sends:
        send.start()

    zero_row = jnp.zeros((ny, packed, LANES), BF16)
    local[0] = zero_row
    local[nx + 1] = zero_row

    def stacked(tile):
        return jnp.concatenate([tile] * halves, axis=0).astype(BF16)

    def spread(tile, y):
        return jnp.broadcast_to(tile[:, y : y + 1], (packed, LANES))

    def total_of(terms):
        while len(terms) > 1:
            terms = [a + b for a, b in zip(terms[::2], terms[1::2])]
        return terms[0]

    def sink(x):
        for g in range(ny // GROUP):
            at = pl.ds(pl.multiple_of(x * ny + g * GROUP, GROUP), GROUP)
            base = pl.multiple_of((x * ny + g * GROUP) * nz, GROUP * nz)
            for h in range(halves):
                lanes = slice(h * LANES, (h + 1) * LANES)
                terms = [adv[h, pl.ds(base + z * GROUP, GROUP), :] * shares[z : z + 1, lanes] for z in range(nz)]
                settled[at, lanes] = total_of(terms)

    share_rows = total // nx

    def two_rows(i, carry):
        for turn in range(2):
            one_row(2 * i + turn)
        return carry

    def one_row(x):
        both = jnp.concatenate([we[x]] * (halves // 2) + [wn[x]] * (halves // 2), axis=0).astype(BF16)
        some = pl.ds(pl.multiple_of(x * share_rows, share_rows), share_rows)
        pz[some, :] = jnp.dot(picks[some, :], table[...], preferred_element_type=F32)
        sink(jnp.maximum(x - 1, 0))

        zero = jnp.zeros((packed, LANES), BF16)
        behind = zero
        centre = local[x + 1, 0]
        for y in range(ny):
            ahead = local[x + 1, y + 1] if y + 1 < ny else zero
            pair = spread(both, y)
            a = jnp.concatenate([pair[0:nz]] * halves, axis=0)
            b = jnp.concatenate([pair[nz : 2 * nz]] * halves, axis=0)
            up_x = jnp.where(a > 0, local[x, y], local[x + 2, y])
            up_y = jnp.where(b > 0, behind, ahead)
            change = jnp.abs(a) * (up_x - centre) + jnp.abs(b) * (up_y - centre)
            value = centre.astype(F32) + change.astype(F32)
            base = pl.multiple_of((x * ny + y - y % GROUP) * nz, GROUP * nz)
            for h in range(halves):
                adv[h, pl.ds(base + y % GROUP, nz, stride=GROUP), :] = value[h * nz : (h + 1) * nz]
            behind, centre = centre, ahead

    for load in small:
        load.wait()

    ratio = fall[...] / (1.0 + fall[...])
    share = jnp.ones((1, bins), F32)
    for z in range(nz):
        share = share * ratio[z : z + 1, :]
        shares[z : z + 1, :] = share
    shares[nz : 2 * nz, :] = ratio
    gain = share

    listed = listed_v[...]
    spots[...] = spot_of(listed // nz, listed % nz, nz)
    spot = pltpu.make_async_copy(spots, cells, spot_sem.at[0])
    spot.start()
    cloudy = target[gx, gy] < plane
    columns = jnp.where(cloudy, listed // nz, -1)
    cloudy_spots = jnp.where(cloudy, spots[...], -1)
    per_tile = LANES // blocks
    for t in range(total // LANES):
        for kept, found in ((ids, columns), (places, cloudy_spots)):
            lines = [found[t * per_tile + i : t * per_tile + i + 1, :] for i in range(per_tile)]
            kept[t : t + 1, :] = jnp.concatenate(lines, axis=1)
    flags = jnp.broadcast_to(jnp.where(cloudy, 1.0, 0.0), (8, blocks)).T
    live[...] = jnp.broadcast_to(flags[:, 0:1], (blocks, LANES))
    heights = (listed % nz).astype(F32).T
    high = shares[0:nz, :].astype(BF16)
    low = (shares[0:nz, :] - high.astype(F32)).astype(BF16)
    table[...] = jnp.concatenate([high, low, jnp.zeros((LANES - 2 * nz, bins), BF16)], axis=0)
    lane = lax.broadcasted_iota(I32, (blocks, LANES), 1)
    level_of = jnp.where(lane < 2 * nz, lane % nz, -1).astype(F32)
    for j in range(width):
        hit = jnp.broadcast_to(heights[:, j : j + 1], (blocks, LANES)) == level_of
        picks[j * blocks : (j + 1) * blocks, :] = jnp.where(hit, 1.0, 0.0).astype(BF16)

    for load in wind_loads:
        load.wait()
    done = 0
    for p in range(parts):
        loads[p].wait()
        upto = nx // 2 if p == parts - 1 else ((p + 1) * per - 1) // 2
        lax.fori_loop(done, upto, two_rows, 0)
        done = upto

    for load in weights:
        load.wait()

    size = min(512, total)
    tile = min(256, pairs)
    inner = down_sem.shape[0] - 2
    span = (nx - 2) // inner
    wide = span * ny

    def gather(i):
        for r in range(i * size, (i + 1) * size):
            cell = pl.ds(cells[r // blocks, r % blocks], 1)
            for h in range(halves):
                rows[h, r : r + 1, :] = adv[h, cell, :]

    def tendency_of(row):
        decline = jnp.dot(row, loss[...], preferred_element_type=F32)
        losses = row.astype(F32) * decline
        gained = jnp.dot(losses.astype(BF16), frag[...], preferred_element_type=F32)
        for n in range(0, pairs, tile):
            first = jnp.dot(row, pair_in[:, n : n + tile], preferred_element_type=F32)
            second = jnp.dot(row, pair_in[:, pairs + n : pairs + n + tile], preferred_element_type=F32)
            product = (first * second).astype(BF16)
            gained = gained + jnp.dot(product, pair_out[n : n + tile, :], preferred_element_type=F32)
        return (gained - losses).astype(BF16).astype(F32)

    def collide(i):
        at = slice(i * size, (i + 1) * size)
        full = jnp.concatenate([rows[h, at, :] for h in range(halves)], axis=1)
        alive = jnp.concatenate([jnp.concatenate([live[...]] * halves, axis=1)] * (size // blocks), axis=0)
        tendency = jnp.where(alive > 0.0, tendency_of(full.astype(BF16)), 0.0)
        q[at, :] = (tendency * pz[at, :]).astype(BF16)
        after = full + tendency
        for h in range(halves):
            moist[h, at, :] = after[:, h * LANES : (h + 1) * LANES]

    def listed_tile(first, apart):
        cell = lax.broadcasted_iota(I32, (GROUP, LANES), 0) * apart + first
        hit = jnp.broadcast_to(places[0:1, :], cell.shape) == cell
        for t in range(1, total // LANES):
            hit = hit | (jnp.broadcast_to(places[t : t + 1, :], cell.shape) == cell)
        found = jnp.max(jnp.where(hit, 1.0, 0.0), axis=1, keepdims=True)
        return jnp.broadcast_to(found, cell.shape)

    def rim_tiles(p):
        if p == inner:
            starts = [x * ny * nz + k * GROUP for x in (0, nx - 1) for k in range(ny * nz // GROUP)]
            return [(start, 1) for start in starts]
        return [(spot_of(x * ny + y, 0, nz), GROUP) for y in (0, ny - 1) for x in range(nx)]

    def collide_rim(p):
        tiles = rim_tiles(p)
        sides = []
        for h in range(halves):
            if p == inner:
                wanted = [adv[h, x * ny * nz : (x + 1) * ny * nz, :] for x in (0, nx - 1)]
            else:
                wanted = [adv[h, pl.ds(first, nz, stride=apart), :] for first, apart in tiles]
            sides.append(jnp.concatenate(wanted, axis=0))
        full = jnp.concatenate(sides, axis=1)
        alive = jnp.concatenate([listed_tile(first, apart) for first, apart in tiles], axis=0)
        alive = jnp.concatenate([alive] * halves, axis=1)
        after = full + jnp.where(alive > 0.0, tendency_of(full.astype(BF16)), 0.0)
        offset = 0 if p == inner else 2 * ny * nz
        for h in range(halves):
            edge_moist[h, offset : offset + full.shape[0], :] = after[:, h * LANES : (h + 1) * LANES]
        left = []
        if p == inner:
            for g in range(2 * ny // GROUP):
                level = [after[(g * nz + z) * GROUP : (g * nz + z + 1) * GROUP, :] * shares[z : z + 1, :] for z in range(nz)]
                left.append(total_of(level))
        else:
            for i in range(2 * nx):
                left.append(jnp.sum(after[i * nz : (i + 1) * nz, :] * shares[0:nz, :], axis=0, keepdims=True))
        edge_flux[edge[p], :] = jnp.concatenate(left, axis=0).astype(BF16)

    def collide_all():
        chunks = total // size
        gather(0)
        for i in range(chunks):
            if i + 1 < chunks:
                gather(i + 1)
            collide(i)

    def collected(column):
        hot = [
            jnp.where(jnp.broadcast_to(ids[t : t + 1, :], column.shape) == column, 1.0, 0.0).astype(BF16)
            for t in range(total // LANES)
        ]
        return jnp.dot(jnp.concatenate(hot, axis=1), q[...], preferred_element_type=F32)

    edge = {inner: slice(0, 2 * ny), inner + 1: slice(2 * ny, 2 * (ny + nx))}

    def down(p):
        src = edge_flux.at[edge[p]] if p in edge else flux.at[pl.ds(p * wide, wide)]
        dst = edge_in.at[edge[p]] if p in edge else arrived.at[pl.ds((1 + p * span) * ny, wide)]
        return pltpu.make_async_remote_copy(
            src_ref=src,
            dst_ref=dst,
            send_sem=down_sem.at[p],
            recv_sem=got_sem.at[p],
            device_id={"gz": jnp.maximum(me - 1, 0)},
            device_id_type=MESH,
        )

    def relay(p):
        down(p).wait_recv()

        @pl.when(me > 0)
        def _():
            if p in edge:
                at = edge[p]
                edge_flux[at, :] = (edge_flux[at, :].astype(F32) + edge_in[at, :].astype(F32) * gain).astype(BF16)
            else:
                at = pl.ds(p * wide, wide)
                got = arrived[pl.ds((1 + p * span) * ny, wide), :].astype(F32)
                flux[at, :] = (flux[at, :].astype(F32) + got * gain).astype(BF16)
            down(p).start()

    spot.wait()
    collide_all()

    for p in range(inner):
        half = wide // 2
        for part in range(2):
            start = p * wide + part * half
            column = lax.broadcasted_iota(I32, (half, LANES), 0) + (ny + start)
            held = settled[ny + start : ny + start + half, :]
            flux[start : start + half, :] = (collected(column) + held).astype(BF16)

        @pl.when(me == top)
        def _():
            down(p).start()

        @pl.when(me == top - 1)
        def _():
            relay(p)

    for send in sends[:2]:
        send.wait_recv()

    def add_halo(column, wind, halo):
        came = wind.astype(F32) * halo.astype(F32)
        at = pl.ds(spot_of(column, 0, nz), nz, stride=GROUP)
        for h in range(halves):
            adv[h, at, :] = adv[h, at, :] + came[h * nz : (h + 1) * nz]

    def edges(x, carry):
        winds = stacked(wn[x])
        add_halo(x * ny, jnp.maximum(spread(winds, 0), 0), south[x])
        add_halo(x * ny + ny - 1, jnp.maximum(-spread(winds, ny - 1), 0), north[x])
        return carry

    lax.fori_loop(0, nx, edges, 0, unroll=8)

    for send, x, halo, sign in ((sends[2], 0, west, 1.0), (sends[3], nx - 1, east, -1.0)):
        send.wait_recv()
        winds = jnp.maximum(sign * stacked(we[x]), 0)
        for y in range(ny):
            add_halo(x * ny + y, spread(winds, y), halo[y])

    for p in edge:
        collide_rim(p)

    @pl.when(me == top)
    def _():
        for p in edge:
            down(p).start()
        arrived[...] = jnp.zeros(arrived.shape, BF16)
        edge_in[...] = jnp.zeros(edge_in.shape, BF16)

    @pl.when(me == top - 1)
    def _():
        for p in edge:
            relay(p)

    @pl.when(me < top - 1)
    def _():
        for p in range(inner + 2):
            relay(p)

    @pl.when(me > 0)
    def _():
        for p in range(inner + 2):
            down(p).wait_send()

    for send in sends:
        send.wait_send()


def settle_kernel(
    adv_in, moist, edge_moist, arrived, edge_in, spots, fall, adv, out, cells, flow, inverse, ratio, level_out, staged,
    cell_sem, out_sem
):
    nx, ny, packed, _ = out.shape
    nz, bins = fall.shape
    halves = bins // LANES
    width, blocks = cells.shape
    slots = level_out.shape[0]
    each = nx // out_sem.shape[0]

    fetch = pltpu.make_async_copy(spots, cells, cell_sem.at[0])
    fetch.start()
    inverse[...] = 1.0 / (1.0 + fall[...])
    ratio[...] = fall[...] * inverse[...]
    flow[...] = arrived[...].astype(F32)
    rim = edge_in[...].astype(F32)
    flow[0:ny, :] = rim[0:ny]
    flow[(nx - 1) * ny : nx * ny, :] = rim[ny : 2 * ny]
    for i in range(nx):
        flow[i * ny : i * ny + 1, :] = rim[2 * ny + i : 2 * ny + i + 1]
        flow[i * ny + ny - 1 : i * ny + ny, :] = rim[2 * ny + nx + i : 2 * ny + nx + i + 1]
    fetch.wait()

    for r in range(width * blocks):
        cell = pl.ds(cells[r // blocks, r % blocks], 1)
        for h in range(halves):
            adv[h, cell, :] = moist[h, r : r + 1, :]

    row = ny * nz
    for h in range(halves):
        for i, x in enumerate((0, nx - 1)):
            adv[h, x * row : (x + 1) * row, :] = edge_moist[h, i * row : (i + 1) * row, :]
        for i, y in enumerate((0, ny - 1)):
            for x in range(nx):
                came = (2 * ny + i * nx + x) * nz
                adv[h, pl.ds(spot_of(x * ny + y, 0, nz), nz, stride=GROUP), :] = edge_moist[h, came : came + nz, :]

    def push(i):
        at = pl.ds(i * each, each)
        return pltpu.make_async_copy(staged.at[at], out.at[at], out_sem.at[i])

    def some_rows(i, carry):
        for slot in range(slots):
            x = i * slots + slot
            for g in range(ny // GROUP):
                column = pl.multiple_of(x * ny + g * GROUP, GROUP)
                for h in range(halves):
                    lanes = slice(h * LANES, (h + 1) * LANES)
                    inflow = flow[pl.ds(column, GROUP), lanes]
                    for z in reversed(range(nz)):
                        held = adv[h, pl.ds(pl.multiple_of(column * nz + z * GROUP, GROUP), GROUP), :] + inflow
                        to = pl.ds(g * GROUP * nz + z, GROUP, stride=nz)
                        level_out[slot, h, to, :] = held * inverse[z : z + 1, lanes]
                        inflow = held * ratio[z : z + 1, lanes]
            for y in range(ny):
                pieces = [level_out[slot, h, y * nz : (y + 1) * nz, :] for h in range(halves)]
                staged[x, y] = jnp.concatenate(pieces, axis=0).astype(BF16)
            if (slot + 1) % each == 0:
                push((x + 1) // each - 1).start()
        return carry

    lax.fori_loop(0, nx // slots, some_rows, 0)
    for i in range(nx // each):
        push(i).wait()


def body(
    spectrum,
    wind_east,
    wind_north,
    fall_rate,
    cloud_cells,
    block_target,
    pair_inputs,
    pair_outputs,
    loss_kernel,
    fragments,
):
    nx, ny, nz, bins = spectrum.shape
    halves = bins // LANES
    cells = nx * ny * nz
    columns = nx * ny
    blocks, width = cloud_cells.shape[3], cloud_cells.shape[4]
    total = blocks * width
    pairs = pair_outputs.shape[0]
    packed = nz * halves
    winds = (wind_east.transpose(0, 2, 1), wind_north.transpose(0, 2, 1))
    listed = cloud_cells.reshape(blocks, width).T
    dma = pltpu.SemaphoreType.DMA
    hbm = pl.BlockSpec(memory_space=pltpu.HBM)
    vmem = pl.BlockSpec(memory_space=pltpu.VMEM)
    dense = spectrum.reshape(nx, ny, nz, halves, LANES).transpose(0, 1, 3, 2, 4).reshape(nx, ny, packed, LANES)
    span = max(s for s in range(1, 6) if (nx - 2) % s == 0)
    inner = (nx - 2) // span
    rim = 2 * (nx + ny)
    parts = 4

    adv, moist, edge_moist, arrived, edge_in, spots, fall_v = pl.pallas_call(
        step_kernel,
        out_shape=(
            pltpu.VMEM((halves, cells, LANES), F32),
            pltpu.VMEM((halves, total, LANES), F32),
            pltpu.VMEM((halves, rim * nz, LANES), F32),
            pltpu.VMEM((columns, bins), BF16),
            pltpu.VMEM((rim, bins), BF16),
            pltpu.VMEM((width, blocks), I32),
            pltpu.VMEM(fall_rate.shape, F32),
        ),
        in_specs=[hbm] * 10,
        out_specs=(vmem,) * 7,
        scratch_shapes=[
            pltpu.VMEM((nx + 2, ny, packed, LANES), BF16),
            pltpu.VMEM(winds[0].shape, F32),
            pltpu.VMEM(winds[1].shape, F32),
            pltpu.VMEM((ny, packed, LANES), BF16),
            pltpu.VMEM((ny, packed, LANES), BF16),
            pltpu.VMEM((nx, packed, LANES), BF16),
            pltpu.VMEM((nx, packed, LANES), BF16),
            pltpu.SMEM((width, blocks), I32),
            pltpu.VMEM((width, blocks), I32),
            pltpu.VMEM(block_target.shape, I32),
            pltpu.VMEM(pair_inputs.shape, BF16),
            pltpu.VMEM(pair_outputs.shape, BF16),
            pltpu.VMEM(loss_kernel.shape, BF16),
            pltpu.VMEM(fragments.shape, BF16),
            pltpu.VMEM((halves, total, LANES), F32),
            pltpu.VMEM((total, bins), BF16),
            pltpu.VMEM((total, bins), F32),
            pltpu.VMEM((max(total // LANES, 8), LANES), I32),
            pltpu.VMEM((max(total // LANES, 8), LANES), I32),
            pltpu.VMEM((blocks, LANES), F32),
            pltpu.VMEM((2 * nz, bins), F32),
            pltpu.VMEM((total, LANES), BF16),
            pltpu.VMEM((LANES, bins), BF16),
            pltpu.VMEM((columns, bins), F32),
            pltpu.VMEM(((nx - 2) * ny, bins), BF16),
            pltpu.VMEM((rim, bins), BF16),
            dma((parts,)),
            dma((10,)),
            dma((1,)),
            dma((4,)),
            dma((4,)),
            dma((inner + 2,)),
            dma((inner + 2,)),
        ],
        compiler_params=pltpu.CompilerParams(
            collective_id=0, has_side_effects=True, vmem_limit_bytes=(60 << 20) - cells * bins * 4
        ),
        name="step",
    )(dense, *winds, fall_rate, listed, block_target, pair_inputs, pair_outputs, loss_kernel, fragments)

    slots = 8
    _, settled = pl.pallas_call(
        settle_kernel,
        out_shape=(
            pltpu.VMEM((halves, cells, LANES), F32),
            jax.ShapeDtypeStruct((nx, ny, packed, LANES), BF16),
        ),
        in_specs=[vmem] * 7,
        out_specs=(vmem, hbm),
        scratch_shapes=[
            pltpu.SMEM((width, blocks), I32),
            pltpu.VMEM((columns, bins), F32),
            pltpu.VMEM((nz, bins), F32),
            pltpu.VMEM((nz, bins), F32),
            pltpu.VMEM((slots, halves, ny * nz, LANES), F32),
            pltpu.VMEM((nx, ny, packed, LANES), BF16),
            dma((1,)),
            dma((nx // 2,)),
        ],
        input_output_aliases={0: 0},
        compiler_params=pltpu.CompilerParams(vmem_limit_bytes=32 << 20),
        name="settle",
    )(adv, moist, edge_moist, arrived, edge_in, spots, fall_v)
    return settled.reshape(nx, ny, halves, nz, LANES).transpose(0, 1, 3, 2, 4).reshape(nx, ny, nz, bins)


def solution(mesh):
    in_specs = (
        P("gx", "gy", "gz", None),
        P("gx", "gy", "gz"),
        P("gx", "gy", "gz"),
        P("gz", None),
        P("gx", "gy", "gz", None, None),
        P(None, None, "gz", None),
        P(),
        P(),
        P(),
        P(),
    )
    out_specs = P("gx", "gy", "gz", None)
    return jax.shard_map(body, mesh=mesh, in_specs=in_specs, out_specs=out_specs, check_vma=False)
```

```python
import functools

import jax
import jax.numpy as jnp
from jax import lax
from jax.experimental import pallas as pl
from jax.experimental.pallas import tpu as pltpu
from jax.sharding import PartitionSpec as P

MESH = pl.DeviceIdType.MESH
F32 = jnp.float32
BF16 = jnp.bfloat16
I32 = jnp.int32
LANES = 128
GROUP = 8


def spot_of(column, level, levels):
    return (column // GROUP * levels + level) * GROUP + column % GROUP


def step_kernel(
    spec, winds_e, winds_n, fall_h, cells_h, target_h, pair_in_h, pair_out_h, loss_h, frag_h,
    adv, moist, edge_moist, arrived, edge_in, spots, fall,
    local, we, wn, west, east, south, north, cells, listed_v, target, pair_in, pair_out, loss, frag,
    rows, q, pz, ids, places, live, shares, picks, table, settled, flux, edge_flux,
    load_sem, in_sem, spot_sem, send_sem, recv_sem, down_sem, got_sem,
):
    nx, ny, packed, _ = spec.shape
    nz, bins = fall.shape
    halves = bins // LANES
    width, blocks = cells.shape
    total = width * blocks
    pairs = pair_out.shape[0]
    parts = load_sem.shape[0]
    per = nx // parts
    gx, gy, me = lax.axis_index("gx"), lax.axis_index("gy"), lax.axis_index("gz")
    sx, sy, count = lax.axis_size("gx"), lax.axis_size("gy"), lax.axis_size("gz")
    plane = sx * sy
    top = count - 1
    to_west = {"gx": lax.rem(gx + sx - 1, sx)}
    to_east = {"gx": lax.rem(gx + 1, sx)}
    to_south = {"gy": lax.rem(gy + sy - 1, sy)}
    to_north = {"gy": lax.rem(gy + 1, sy)}
    above = {"gz": lax.rem(me + 1, count)}
    below = {"gz": lax.rem(me + top, count)}

    barrier = pltpu.get_barrier_semaphore()
    for peer in (to_west, to_east, to_south, to_north, above, below):
        pl.semaphore_signal(barrier, inc=1, device_id=peer, device_id_type=MESH)

    def fetch(i, src, dst):
        return pltpu.make_async_copy(src, dst, in_sem.at[i])

    wind_loads = [fetch(0, winds_e, we), fetch(1, winds_n, wn)]
    loads = [
        pltpu.make_async_copy(spec.at[pl.ds(p * per, per)], local.at[pl.ds(1 + p * per, per)], load_sem.at[p])
        for p in range(parts)
    ]
    small = [fetch(2, fall_h, fall), fetch(3, cells_h, listed_v), fetch(4, target_h, target)]
    weights = [
        fetch(6, pair_in_h, pair_in), fetch(7, pair_out_h, pair_out), fetch(8, loss_h, loss), fetch(9, frag_h, frag)
    ]
    for load in small + wind_loads + loads + weights:
        load.start()
    pl.semaphore_wait(barrier, 6)

    sends = [
        pltpu.make_async_remote_copy(
            src_ref=src,
            dst_ref=dst,
            send_sem=send_sem.at[i],
            recv_sem=recv_sem.at[i],
            device_id=peer,
            device_id_type=MESH,
        )
        for i, (src, dst, peer) in enumerate(
            (
                (spec.at[:, ny - 1], south, to_north),
                (spec.at[:, 0], north, to_south),
                (spec.at[nx - 1], west, to_east),
                (spec.at[0], east, to_west),
            )
        )
    ]
    for send in sends:
        send.start()

    zero_row = jnp.zeros((ny, packed, LANES), BF16)
    local[0] = zero_row
    local[nx + 1] = zero_row

    def stacked(tile):
        return jnp.concatenate([tile] * halves, axis=0).astype(BF16)

    def spread(tile, y):
        return jnp.broadcast_to(tile[:, y : y + 1], (packed, LANES))

    def total_of(terms):
        while len(terms) > 1:
            terms = [a + b for a, b in zip(terms[::2], terms[1::2])]
        return terms[0]

    def sink(x):
        for g in range(ny // GROUP):
            at = pl.ds(pl.multiple_of(x * ny + g * GROUP, GROUP), GROUP)
            base = pl.multiple_of((x * ny + g * GROUP) * nz, GROUP * nz)
            for h in range(halves):
                lanes = slice(h * LANES, (h + 1) * LANES)
                terms = [adv[h, pl.ds(base + z * GROUP, GROUP), :] * shares[z : z + 1, lanes] for z in range(nz)]
                settled[at, lanes] = total_of(terms)

    share_rows = total // nx

    def two_rows(i, carry):
        for turn in range(2):
            one_row(2 * i + turn)
        return carry

    def one_row(x):
        both = jnp.concatenate([we[x]] * (halves // 2) + [wn[x]] * (halves // 2), axis=0).astype(BF16)
        some = pl.ds(pl.multiple_of(x * share_rows, share_rows), share_rows)
        pz[some, :] = jnp.dot(picks[some, :], table[...], preferred_element_type=F32)
        sink(jnp.maximum(x - 1, 0))

        zero = jnp.zeros((packed, LANES), BF16)
        behind = zero
        centre = local[x + 1, 0]
        for y in range(ny):
            ahead = local[x + 1, y + 1] if y + 1 < ny else zero
            pair = spread(both, y)
            a = jnp.concatenate([pair[0:nz]] * halves, axis=0)
            b = jnp.concatenate([pair[nz : 2 * nz]] * halves, axis=0)
            up_x = jnp.where(a > 0, local[x, y], local[x + 2, y])
            up_y = jnp.where(b > 0, behind, ahead)
            change = jnp.abs(a) * (up_x - centre) + jnp.abs(b) * (up_y - centre)
            value = centre.astype(F32) + change.astype(F32)
            base = pl.multiple_of((x * ny + y - y % GROUP) * nz, GROUP * nz)
            for h in range(halves):
                adv[h, pl.ds(base + y % GROUP, nz, stride=GROUP), :] = value[h * nz : (h + 1) * nz]
            behind, centre = centre, ahead

    for load in small:
        load.wait()

    ratio = fall[...] / (1.0 + fall[...])
    share = jnp.ones((1, bins), F32)
    for z in range(nz):
        share = share * ratio[z : z + 1, :]
        shares[z : z + 1, :] = share
    shares[nz : 2 * nz, :] = ratio
    gain = share

    listed = listed_v[...]
    spots[...] = spot_of(listed // nz, listed % nz, nz)
    spot = pltpu.make_async_copy(spots, cells, spot_sem.at[0])
    spot.start()
    cloudy = target[gx, gy] < plane
    columns = jnp.where(cloudy, listed // nz, -1)
    cloudy_spots = jnp.where(cloudy, spots[...], -1)
    per_tile = LANES // blocks
    for t in range(total // LANES):
        for kept, found in ((ids, columns), (places, cloudy_spots)):
            lines = [found[t * per_tile + i : t * per_tile + i + 1, :] for i in range(per_tile)]
            kept[t : t + 1, :] = jnp.concatenate(lines, axis=1)
    flags = jnp.broadcast_to(jnp.where(cloudy, 1.0, 0.0), (8, blocks)).T
    live[...] = jnp.broadcast_to(flags[:, 0:1], (blocks, LANES))
    heights = (listed % nz).astype(F32).T
    high = shares[0:nz, :].astype(BF16)
    low = (shares[0:nz, :] - high.astype(F32)).astype(BF16)
    table[...] = jnp.concatenate([high, low, jnp.zeros((LANES - 2 * nz, bins), BF16)], axis=0)
    lane = lax.broadcasted_iota(I32, (blocks, LANES), 1)
    level_of = jnp.where(lane < 2 * nz, lane % nz, -1).astype(F32)
    for j in range(width):
        hit = jnp.broadcast_to(heights[:, j : j + 1], (blocks, LANES)) == level_of
        picks[j * blocks : (j + 1) * blocks, :] = jnp.where(hit, 1.0, 0.0).astype(BF16)

    for load in wind_loads:
        load.wait()
    done = 0
    for p in range(parts):
        loads[p].wait()
        upto = nx // 2 if p == parts - 1 else ((p + 1) * per - 1) // 2
        lax.fori_loop(done, upto, two_rows, 0)
        done = upto

    for load in weights:
        load.wait()

    size = min(512, total)
    tile = min(256, pairs)
    inner = down_sem.shape[0] - 2
    span = (nx - 2) // inner
    wide = span * ny

    def gather(i):
        for r in range(i * size, (i + 1) * size):
            cell = pl.ds(cells[r // blocks, r % blocks], 1)
            for h in range(halves):
                rows[h, r : r + 1, :] = adv[h, cell, :]

    def tendency_of(row):
        decline = jnp.dot(row, loss[...], preferred_element_type=F32)
        losses = row.astype(F32) * decline
        gained = jnp.dot(losses.astype(BF16), frag[...], preferred_element_type=F32)
        for n in range(0, pairs, tile):
            first = jnp.dot(row, pair_in[:, n : n + tile], preferred_element_type=F32)
            second = jnp.dot(row, pair_in[:, pairs + n : pairs + n + tile], preferred_element_type=F32)
            product = (first * second).astype(BF16)
            gained = gained + jnp.dot(product, pair_out[n : n + tile, :], preferred_element_type=F32)
        return (gained - losses).astype(BF16).astype(F32)

    def collide(i):
        at = slice(i * size, (i + 1) * size)
        full = jnp.concatenate([rows[h, at, :] for h in range(halves)], axis=1)
        alive = jnp.concatenate([jnp.concatenate([live[...]] * halves, axis=1)] * (size // blocks), axis=0)
        tendency = jnp.where(alive > 0.0, tendency_of(full.astype(BF16)), 0.0)
        q[at, :] = (tendency * pz[at, :]).astype(BF16)
        after = full + tendency
        for h in range(halves):
            moist[h, at, :] = after[:, h * LANES : (h + 1) * LANES]

    def listed_tile(first, apart):
        cell = lax.broadcasted_iota(I32, (GROUP, LANES), 0) * apart + first
        hit = jnp.broadcast_to(places[0:1, :], cell.shape) == cell
        for t in range(1, total // LANES):
            hit = hit | (jnp.broadcast_to(places[t : t + 1, :], cell.shape) == cell)
        found = jnp.max(jnp.where(hit, 1.0, 0.0), axis=1, keepdims=True)
        return jnp.broadcast_to(found, cell.shape)

    def rim_tiles(p):
        if p == inner:
            starts = [x * ny * nz + k * GROUP for x in (0, nx - 1) for k in range(ny * nz // GROUP)]
            return [(start, 1) for start in starts]
        return [(spot_of(x * ny + y, 0, nz), GROUP) for y in (0, ny - 1) for x in range(nx)]

    def collide_rim(p):
        tiles = rim_tiles(p)
        sides = []
        for h in range(halves):
            if p == inner:
                wanted = [adv[h, x * ny * nz : (x + 1) * ny * nz, :] for x in (0, nx - 1)]
            else:
                wanted = [adv[h, pl.ds(first, nz, stride=apart), :] for first, apart in tiles]
            sides.append(jnp.concatenate(wanted, axis=0))
        full = jnp.concatenate(sides, axis=1)
        alive = jnp.concatenate([listed_tile(first, apart) for first, apart in tiles], axis=0)
        alive = jnp.concatenate([alive] * halves, axis=1)
        after = full + jnp.where(alive > 0.0, tendency_of(full.astype(BF16)), 0.0)
        offset = 0 if p == inner else 2 * ny * nz
        for h in range(halves):
            edge_moist[h, offset : offset + full.shape[0], :] = after[:, h * LANES : (h + 1) * LANES]
        left = []
        if p == inner:
            for g in range(2 * ny // GROUP):
                level = [after[(g * nz + z) * GROUP : (g * nz + z + 1) * GROUP, :] * shares[z : z + 1, :] for z in range(nz)]
                left.append(total_of(level))
        else:
            for i in range(2 * nx):
                left.append(jnp.sum(after[i * nz : (i + 1) * nz, :] * shares[0:nz, :], axis=0, keepdims=True))
        edge_flux[edge[p], :] = jnp.concatenate(left, axis=0).astype(BF16)

    def collide_all():
        chunks = total // size
        gather(0)
        for i in range(chunks):
            if i + 1 < chunks:
                gather(i + 1)
            collide(i)

    def collected(column):
        hot = [
            jnp.where(jnp.broadcast_to(ids[t : t + 1, :], column.shape) == column, 1.0, 0.0).astype(BF16)
            for t in range(total // LANES)
        ]
        return jnp.dot(jnp.concatenate(hot, axis=1), q[...], preferred_element_type=F32)

    edge = {inner: slice(0, 2 * ny), inner + 1: slice(2 * ny, 2 * (ny + nx))}

    def down(p):
        src = edge_flux.at[edge[p]] if p in edge else flux.at[pl.ds(p * wide, wide)]
        dst = edge_in.at[edge[p]] if p in edge else arrived.at[pl.ds((1 + p * span) * ny, wide)]
        return pltpu.make_async_remote_copy(
            src_ref=src,
            dst_ref=dst,
            send_sem=down_sem.at[p],
            recv_sem=got_sem.at[p],
            device_id={"gz": jnp.maximum(me - 1, 0)},
            device_id_type=MESH,
        )

    def relay(p):
        down(p).wait_recv()

        @pl.when(me > 0)
        def _():
            if p in edge:
                at = edge[p]
                edge_flux[at, :] = (edge_flux[at, :].astype(F32) + edge_in[at, :].astype(F32) * gain).astype(BF16)
            else:
                at = pl.ds(p * wide, wide)
                got = arrived[pl.ds((1 + p * span) * ny, wide), :].astype(F32)
                flux[at, :] = (flux[at, :].astype(F32) + got * gain).astype(BF16)
            down(p).start()

    spot.wait()
    collide_all()

    for p in range(inner):
        half = wide // 2
        for part in range(2):
            start = p * wide + part * half
            column = lax.broadcasted_iota(I32, (half, LANES), 0) + (ny + start)
            held = settled[ny + start : ny + start + half, :]
            flux[start : start + half, :] = (collected(column) + held).astype(BF16)

        @pl.when(me == top)
        def _():
            down(p).start()

        @pl.when(me == top - 1)
        def _():
            relay(p)

    for send in sends[:2]:
        send.wait_recv()

    def add_halo(column, wind, halo):
        came = wind.astype(F32) * halo.astype(F32)
        at = pl.ds(spot_of(column, 0, nz), nz, stride=GROUP)
        for h in range(halves):
            adv[h, at, :] = adv[h, at, :] + came[h * nz : (h + 1) * nz]

    def edges(x, carry):
        winds = stacked(wn[x])
        add_halo(x * ny, jnp.maximum(spread(winds, 0), 0), south[x])
        add_halo(x * ny + ny - 1, jnp.maximum(-spread(winds, ny - 1), 0), north[x])
        return carry

    lax.fori_loop(0, nx, edges, 0, unroll=8)

    for send, x, halo, sign in ((sends[2], 0, west, 1.0), (sends[3], nx - 1, east, -1.0)):
        send.wait_recv()
        winds = jnp.maximum(sign * stacked(we[x]), 0)
        for y in range(ny):
            add_halo(x * ny + y, spread(winds, y), halo[y])

    for p in edge:
        collide_rim(p)

    @pl.when(me == top)
    def _():
        for p in edge:
            down(p).start()
        arrived[...] = jnp.zeros(arrived.shape, BF16)
        edge_in[...] = jnp.zeros(edge_in.shape, BF16)

    @pl.when(me == top - 1)
    def _():
        for p in edge:
            relay(p)

    @pl.when(me < top - 1)
    def _():
        for p in range(inner + 2):
            relay(p)

    @pl.when(me > 0)
    def _():
        for p in range(inner + 2):
            down(p).wait_send()

    for send in sends:
        send.wait_send()


def settle_kernel(
    adv_in, moist, edge_moist, arrived, edge_in, spots, fall, adv, out, cells, flow, inverse, ratio, level_out, staged,
    cell_sem, out_sem
):
    nx, ny, packed, _ = out.shape
    nz, bins = fall.shape
    halves = bins // LANES
    width, blocks = cells.shape
    slots = level_out.shape[0]
    each = nx // out_sem.shape[0]

    fetch = pltpu.make_async_copy(spots, cells, cell_sem.at[0])
    fetch.start()
    inverse[...] = 1.0 / (1.0 + fall[...])
    ratio[...] = fall[...] * inverse[...]
    flow[...] = arrived[...].astype(F32)
    rim = edge_in[...].astype(F32)
    flow[0:ny, :] = rim[0:ny]
    flow[(nx - 1) * ny : nx * ny, :] = rim[ny : 2 * ny]
    for i in range(nx):
        flow[i * ny : i * ny + 1, :] = rim[2 * ny + i : 2 * ny + i + 1]
        flow[i * ny + ny - 1 : i * ny + ny, :] = rim[2 * ny + nx + i : 2 * ny + nx + i + 1]
    fetch.wait()

    for r in range(width * blocks):
        cell = pl.ds(cells[r // blocks, r % blocks], 1)
        for h in range(halves):
            adv[h, cell, :] = moist[h, r : r + 1, :]

    row = ny * nz
    for h in range(halves):
        for i, x in enumerate((0, nx - 1)):
            adv[h, x * row : (x + 1) * row, :] = edge_moist[h, i * row : (i + 1) * row, :]
        for i, y in enumerate((0, ny - 1)):
            for x in range(nx):
                came = (2 * ny + i * nx + x) * nz
                adv[h, pl.ds(spot_of(x * ny + y, 0, nz), nz, stride=GROUP), :] = edge_moist[h, came : came + nz, :]

    def push(i):
        at = pl.ds(i * each, each)
        return pltpu.make_async_copy(staged.at[at], out.at[at], out_sem.at[i])

    def some_rows(i, carry):
        for slot in range(slots):
            x = i * slots + slot
            for g in range(ny // GROUP):
                column = pl.multiple_of(x * ny + g * GROUP, GROUP)
                for h in range(halves):
                    lanes = slice(h * LANES, (h + 1) * LANES)
                    inflow = flow[pl.ds(column, GROUP), lanes]
                    for z in reversed(range(nz)):
                        held = adv[h, pl.ds(pl.multiple_of(column * nz + z * GROUP, GROUP), GROUP), :] + inflow
                        to = pl.ds(g * GROUP * nz + z, GROUP, stride=nz)
                        level_out[slot, h, to, :] = held * inverse[z : z + 1, lanes]
                        inflow = held * ratio[z : z + 1, lanes]
            for y in range(ny):
                pieces = [level_out[slot, h, y * nz : (y + 1) * nz, :] for h in range(halves)]
                staged[x, y] = jnp.concatenate(pieces, axis=0).astype(BF16)
            if (slot + 1) % each == 0:
                push((x + 1) // each - 1).start()
        return carry

    lax.fori_loop(0, nx // slots, some_rows, 0)
    for i in range(nx // each):
        push(i).wait()


def body(
    spectrum,
    wind_east,
    wind_north,
    fall_rate,
    cloud_cells,
    block_target,
    pair_inputs,
    pair_outputs,
    loss_kernel,
    fragments,
):
    nx, ny, nz, bins = spectrum.shape
    halves = bins // LANES
    cells = nx * ny * nz
    columns = nx * ny
    blocks, width = cloud_cells.shape[3], cloud_cells.shape[4]
    total = blocks * width
    pairs = pair_outputs.shape[0]
    packed = nz * halves
    winds = (wind_east.transpose(0, 2, 1), wind_north.transpose(0, 2, 1))
    listed = cloud_cells.reshape(blocks, width).T
    dma = pltpu.SemaphoreType.DMA
    hbm = pl.BlockSpec(memory_space=pltpu.HBM)
    vmem = pl.BlockSpec(memory_space=pltpu.VMEM)
    dense = spectrum.reshape(nx, ny, nz, halves, LANES).transpose(0, 1, 3, 2, 4).reshape(nx, ny, packed, LANES)
    span = max(s for s in range(1, 6) if (nx - 2) % s == 0)
    inner = (nx - 2) // span
    rim = 2 * (nx + ny)
    parts = 4

    adv, moist, edge_moist, arrived, edge_in, spots, fall_v = pl.pallas_call(
        step_kernel,
        out_shape=(
            pltpu.VMEM((halves, cells, LANES), F32),
            pltpu.VMEM((halves, total, LANES), F32),
            pltpu.VMEM((halves, rim * nz, LANES), F32),
            pltpu.VMEM((columns, bins), BF16),
            pltpu.VMEM((rim, bins), BF16),
            pltpu.VMEM((width, blocks), I32),
            pltpu.VMEM(fall_rate.shape, F32),
        ),
        in_specs=[hbm] * 10,
        out_specs=(vmem,) * 7,
        scratch_shapes=[
            pltpu.VMEM((nx + 2, ny, packed, LANES), BF16),
            pltpu.VMEM(winds[0].shape, F32),
            pltpu.VMEM(winds[1].shape, F32),
            pltpu.VMEM((ny, packed, LANES), BF16),
            pltpu.VMEM((ny, packed, LANES), BF16),
            pltpu.VMEM((nx, packed, LANES), BF16),
            pltpu.VMEM((nx, packed, LANES), BF16),
            pltpu.SMEM((width, blocks), I32),
            pltpu.VMEM((width, blocks), I32),
            pltpu.VMEM(block_target.shape, I32),
            pltpu.VMEM(pair_inputs.shape, BF16),
            pltpu.VMEM(pair_outputs.shape, BF16),
            pltpu.VMEM(loss_kernel.shape, BF16),
            pltpu.VMEM(fragments.shape, BF16),
            pltpu.VMEM((halves, total, LANES), F32),
            pltpu.VMEM((total, bins), BF16),
            pltpu.VMEM((total, bins), F32),
            pltpu.VMEM((max(total // LANES, 8), LANES), I32),
            pltpu.VMEM((max(total // LANES, 8), LANES), I32),
            pltpu.VMEM((blocks, LANES), F32),
            pltpu.VMEM((2 * nz, bins), F32),
            pltpu.VMEM((total, LANES), BF16),
            pltpu.VMEM((LANES, bins), BF16),
            pltpu.VMEM((columns, bins), F32),
            pltpu.VMEM(((nx - 2) * ny, bins), BF16),
            pltpu.VMEM((rim, bins), BF16),
            dma((parts,)),
            dma((10,)),
            dma((1,)),
            dma((4,)),
            dma((4,)),
            dma((inner + 2,)),
            dma((inner + 2,)),
        ],
        compiler_params=pltpu.CompilerParams(
            collective_id=0, has_side_effects=True, vmem_limit_bytes=(60 << 20) - cells * bins * 4
        ),
        name="step",
    )(dense, *winds, fall_rate, listed, block_target, pair_inputs, pair_outputs, loss_kernel, fragments)

    slots = 8
    _, settled = pl.pallas_call(
        settle_kernel,
        out_shape=(
            pltpu.VMEM((halves, cells, LANES), F32),
            jax.ShapeDtypeStruct((nx, ny, packed, LANES), BF16),
        ),
        in_specs=[vmem] * 7,
        out_specs=(vmem, hbm),
        scratch_shapes=[
            pltpu.SMEM((width, blocks), I32),
            pltpu.VMEM((columns, bins), F32),
            pltpu.VMEM((nz, bins), F32),
            pltpu.VMEM((nz, bins), F32),
            pltpu.VMEM((slots, halves, ny * nz, LANES), F32),
            pltpu.VMEM((nx, ny, packed, LANES), BF16),
            dma((1,)),
            dma((nx // 4,)),
        ],
        input_output_aliases={0: 0},
        compiler_params=pltpu.CompilerParams(vmem_limit_bytes=32 << 20),
        name="settle",
    )(adv, moist, edge_moist, arrived, edge_in, spots, fall_v)
    return settled.reshape(nx, ny, halves, nz, LANES).transpose(0, 1, 3, 2, 4).reshape(nx, ny, nz, bins)


def solution(mesh):
    in_specs = (
        P("gx", "gy", "gz", None),
        P("gx", "gy", "gz"),
        P("gx", "gy", "gz"),
        P("gz", None),
        P("gx", "gy", "gz", None, None),
        P(None, None, "gz", None),
        P(),
        P(),
        P(),
        P(),
    )
    out_specs = P("gx", "gy", "gz", None)
    return jax.shard_map(body, mesh=mesh, in_specs=in_specs, out_specs=out_specs, check_vma=False)
```
